32 devices in a mesh: seq: 4 (over y, x), dp: 8 (over z, core).
Axes of the slice: x: 2, y: 2, z: 4, core: 2. Of those that a mesh axis runs over, the one named last changes fastest.
Arguments:
- tokens: bfloat16 [24, 208, 768], P('dp', 'seq'), may hold values from -6 to 6
- key_mask: int32 [24, 208], P('dp'), may hold values 0 or 1
- prompts: float32 [50, 768], replicated, may hold values from -6 to 6
- gain_one: float32 [768], replicated, may hold values from 0.1 to 1.9
- shift_one: float32 [768], replicated, may hold values from -3 to 3
- w_qkv: bfloat16 [768, 2304], replicated, may hold values from -0.21875 to 0.21875
- b_qkv: float32 [2304], replicated, may hold values from -3 to 3
- w_out: bfloat16 [768, 768], replicated, may hold values from -0.875 to 0.875
- b_out: float32 [768], replicated, may hold values from -2 to 2
- gain_two: float32 [768], replicated, may hold values from 0.1 to 1.9
- shift_two: float32 [768], replicated, may hold values from -3 to 3
- w_up: bfloat16 [768, 3072], replicated, may hold values from -0.21875 to 0.21875
- b_up: float32 [3072], replicated, may hold values from -3 to 3
- w_down: bfloat16 [3072, 768], replicated, may hold values from -0.109375 to 0.109375
- b_down: float32 [768], replicated, may hold values from -2 to 2
- cotangent: bfloat16 [24, 208, 768], P('dp', 'seq'), may hold values from -6 to 6
- start_factor: float32 [768, 8], replicated, may hold values from -6 to 6
- error_buffer: float32 [8, 50, 768], P('dp'), may hold values from -12 to 12
- momentum: float32 [50, 768], replicated, may hold values from -0.875 to 0.875
Outputs:
- layer_out: bfloat16 [24, 208, 768], P('dp', 'seq')
- input_grad: bfloat16 [24, 208, 768], P('dp', 'seq')
- left_basis: float32 [50, 8], replicated
- right_sum: float32 [768, 8], replicated
- new_error: float32 [8, 50, 768], P('dp')
- new_momentum: float32 [50, 768], replicated
- new_prompts: float32 [50, 768], replicated
- prompt_copy: bfloat16 [50, 768], replicated
The draws below stay inside these ranges and needn't reach their ends.
All inputs are finite; a program needn't handle non-finite values. No bound on the sum of `key_mask` on one device may be relied on, other than what follows from the above.
Results may differ from the reference program's by a relative error of at most 0.015.
Values may be sent and summed in bfloat16 or wider, within the bound.
No kernel may reach another device: no remote copies, remote signals or barrier semaphores. Data moves between devices by JAX's collectives and lax.ppermute only.
A program may use at most 64 MiB of HBM per device.

```python
import math
import jax
import jax.numpy as jnp
from jax import lax

D = 768
HEADS = 12
FF = 3072
PROMPTS = 50
ROWS = 208
RANK = 8
IMAGES = 24
N_DP = 8


def place_ends(result, own_key, low, top_value):
    index_at = [jax.random.randint(jax.random.fold_in(own_key, axis), (), 0, length) for axis, length in enumerate(result.shape)]
    longest = result.shape.index(max(result.shape))
    beside = index_at[:longest] + [(index_at[longest] + 1) % result.shape[longest]] + index_at[longest + 1:]
    return result.at[tuple(index_at)].set(low).at[tuple(beside)].set(top_value)


def block_scale(rng, extent, cuts, smallest, top_value):
    def one(dim, parts):
        draws = jax.random.uniform(jax.random.fold_in(jax.random.fold_in(rng, 6), dim), (parts,), jnp.float32, smallest / len(cuts), top_value / len(cuts))
        return jnp.repeat(jnp.exp(draws), extent[dim] // parts).reshape((-1,) + (1,) * (len(extent) - dim - 1))

    level = one(*cuts[0])
    for cut in cuts[1:]:
        level = level * one(*cut)
    return level


def normal_values(stream_key, shape, scale, reach, pieces=(), kind=jnp.bfloat16):
    level = block_scale(stream_key, shape, pieces, -0.22, 0.18) if pieces else 1.0
    result = jax.random.normal(stream_key, shape, jnp.float32) * scale * level
    return jnp.minimum(jnp.maximum(result, -reach), reach).astype(kind)


def setup_inputs(seed: int = 0) -> dict:
    key_of = jax.random.split(jax.random.key(seed), 20)
    tokens = normal_values(key_of[0], (IMAGES, ROWS, D), 1.0, 6.0, ((0, 8), (1, 4)))
    key_mask = place_ends((jax.random.randint(key_of[1], (IMAGES, ROWS), 0, 8) < 7).astype(jnp.int32), jax.random.fold_in(key_of[1], 1), 0, 1)
    prompts = normal_values(key_of[2], (PROMPTS, D), 1.0, 6.0, (), jnp.float32)
    gain_one = jnp.clip(1.0 + 0.18 * jax.random.normal(key_of[3], (D,), jnp.float32), 0.1, 1.9)
    shift_one = normal_values(key_of[4], (D,), 0.5, 3.0, (), jnp.float32)
    w_qkv = normal_values(key_of[5], (D, 3 * D), D ** -0.5, 0.21875)
    b_qkv = normal_values(key_of[6], (3 * D,), 0.5, 3.0, (), jnp.float32)
    w_out = normal_values(key_of[7], (D, D), (D // 16) ** -0.5, 0.875)
    b_out = normal_values(key_of[8], (D,), 0.3, 2.0, (), jnp.float32)
    gain_two = jnp.clip(1.0 + 0.18 * jax.random.normal(key_of[9], (D,), jnp.float32), 0.1, 1.9)
    shift_two = normal_values(key_of[10], (D,), 0.5, 3.0, (), jnp.float32)
    w_up = normal_values(key_of[11], (D, FF), D ** -0.5, 0.21875)
    b_up = normal_values(key_of[12], (FF,), 0.5, 3.0, (), jnp.float32)
    w_down = normal_values(key_of[13], (FF, D), FF ** -0.5, 0.109375)
    b_down = normal_values(key_of[14], (D,), 0.3, 2.0, (), jnp.float32)
    cotangent = normal_values(key_of[15], (IMAGES, ROWS, D), 1.0, 6.0, ((0, 8), (1, 4)))
    start_factor = normal_values(key_of[16], (D, RANK), 1.0, 6.0, (), jnp.float32)
    error_buffer = normal_values(key_of[17], (N_DP, PROMPTS, D), 2.0, 12.0, ((0, 8),), jnp.float32)
    momentum = normal_values(key_of[18], (PROMPTS, D), (0.3 / IMAGES ** 0.5), 0.875, (), jnp.float32)
    return dict(tokens=tokens, key_mask=key_mask, prompts=prompts, gain_one=gain_one, shift_one=shift_one, w_qkv=w_qkv, b_qkv=b_qkv, w_out=w_out, b_out=b_out, gain_two=gain_two, shift_two=shift_two, w_up=w_up, b_up=b_up, w_down=w_down, b_down=b_down, cotangent=cotangent, start_factor=start_factor, error_buffer=error_buffer, momentum=momentum)


highest = lax.Precision.HIGHEST
norm_eps = 1e-06
momentum_decay = 0.5
rate_scale = 3.0

@jax.custom_vjp
def low(v):
    return lax.optimization_barrier(v.astype(jnp.bfloat16)).astype(jnp.float32)

@jax.custom_vjp
def low_back(v):
    return v

def low_keep(v):
    return (low(v), None)

def low_pass(kept, grad):
    return (grad,)

def back_keep(v):
    return (v, None)

def back_low(kept, grad):
    return (low(grad),)
low.defvjp(low_keep, low_pass)
low_back.defvjp(back_keep, back_low)

def layer_norm(values, gain, shift):
    center = values - lax.optimization_barrier(jnp.mean(values, axis=-1, keepdims=True))
    spread = lax.optimization_barrier(jnp.mean(center * center, axis=-1, keepdims=True))
    return center * lax.rsqrt(spread + norm_eps) * gain + shift

def matmul(left, right):
    return jnp.matmul(left, right, precision=highest)

def forward(prompt_rows, rows, valid, params):
    gain_one, shift_one, w_qkv, b_qkv, w_out, b_out, gain_two, shift_two, w_up, b_up, w_down, b_down = params
    images, length, width = rows.shape
    head = width // HEADS
    normed_prompt = low(layer_norm(prompt_rows, gain_one, shift_one))
    prompt_kv = low(matmul(normed_prompt, w_qkv[:, width:]) + b_qkv[width:])
    normed = low(layer_norm(rows, gain_one, shift_one))
    qkv = low(low_back(matmul(normed, w_qkv) + b_qkv))
    query = qkv[..., :width].reshape(images, length, HEADS, head)
    key_rows = qkv[..., width:2 * width].reshape(images, length, HEADS, head)
    value_rows = qkv[..., 2 * width:].reshape(images, length, HEADS, head)
    key_prompt = prompt_kv[:, :width].reshape(PROMPTS, HEADS, head)
    value_prompt = prompt_kv[:, width:].reshape(PROMPTS, HEADS, head)
    raw = jnp.concatenate([jnp.einsum('bqhd,khd->bhqk', query, key_prompt, precision=highest), jnp.einsum('bqhd,bkhd->bhqk', query, key_rows, precision=highest)], -1)
    raw = low_back(raw)
    keep = jnp.concatenate([jnp.ones((images, PROMPTS), bool), valid == 1], -1)[:, None, None, :]
    scores = jnp.where(keep, raw * head ** (-0.5), -jnp.inf)
    weights = low(jax.nn.softmax(scores, axis=-1))
    mixed = jnp.einsum('bhqk,khd->bqhd', weights[..., :PROMPTS], value_prompt, precision=highest)
    mixed = mixed + jnp.einsum('bhqk,bkhd->bqhd', weights[..., PROMPTS:], value_rows, precision=highest)
    mixed = low(low_back(mixed.reshape(images, length, width)))
    attn = low_back(matmul(mixed, w_out) + b_out)
    resid = rows + attn
    normed_two = low(layer_norm(resid, gain_two, shift_two))
    hidden = low_back(matmul(normed_two, w_up) + b_up)
    act = low(jax.nn.gelu(hidden, approximate=False))
    branch = low_back(matmul(act, w_down) + b_down)
    return resid + branch

def orthonormal(matrix):
    columns = []
    for index in range(matrix.shape[1]):
        column = matrix[:, index]
        for earlier in columns:
            column = column - jnp.sum(earlier * column) * earlier
        column = column * lax.rsqrt(jnp.sum(column * column) + 1e-12)
        columns.append(column)
    return jnp.stack(columns, 1)

def reference(tokens, key_mask, prompts, gain_one, shift_one, w_qkv, b_qkv, w_out, b_out, gain_two, shift_two, w_up, b_up, w_down, b_down, cotangent, start_factor, error_buffer, momentum):
    params = tuple((p.astype(jnp.float32) for p in (gain_one, shift_one, w_qkv, b_qkv, w_out, b_out, gain_two, shift_two, w_up, b_up, w_down, b_down)))
    prompt_rows = low(prompts.astype(jnp.float32))
    workers = error_buffer.shape[0]
    width = tokens.shape[-1]

    def one_worker(items):
        rows, valid, grad_out = items
        outputs, pullback = jax.vjp(lambda p, r: forward(p, r, valid, params), prompt_rows, rows.astype(jnp.float32))
        grad_prompt, grad_rows = pullback(grad_out.astype(jnp.float32))
        return (outputs.astype(jnp.bfloat16), grad_rows.astype(jnp.bfloat16), grad_prompt)
    layer_out, input_grad, grads = lax.map(one_worker, (tokens.reshape(workers, -1, ROWS, width), key_mask.reshape(workers, -1, ROWS), cotangent.reshape(workers, -1, ROWS, width)))
    combined = grads + error_buffer
    left = lax.optimization_barrier(jnp.sum(jnp.einsum('wpd,dr->wpr', combined, start_factor, precision=highest), 0))
    left_basis = orthonormal(left)
    right = jnp.einsum('wpd,pr->wdr', combined, left_basis, precision=highest)
    right_sum = lax.optimization_barrier(jnp.sum(right, 0))
    new_error = combined - jnp.einsum('pr,wdr->wpd', left_basis, right, precision=highest)
    update = matmul(left_basis, right_sum.T) / IMAGES
    new_momentum = momentum_decay * momentum + update
    new_prompts = prompts - rate_scale * math.sqrt(IMAGES) * new_momentum
    return (layer_out.reshape(tokens.shape), input_grad.reshape(tokens.shape), left_basis, right_sum, new_error, new_momentum, new_prompts, new_prompts.astype(jnp.bfloat16))
```

```python
import functools
import math

import jax
import jax.numpy as jnp
from jax import lax
from jax.experimental import pallas as pl
from jax.experimental.pallas import tpu as pltpu
from jax.sharding import PartitionSpec as P

HEADS = 12
EPS = 1e-06
MOMENTUM_DECAY = 0.5
RATE_SCALE = 3.0
HIGHEST = lax.Precision.HIGHEST
F32 = jnp.float32
BF16 = jnp.bfloat16
VMEM = pl.BlockSpec(memory_space=pltpu.VMEM)
ANY = pl.BlockSpec(memory_space=pl.ANY)
MIB = 1 << 20
LOG2E = 1.4426950408889634


def up(value, unit):
    return -(-value // unit) * unit


def dot(a, b):
    return jnp.dot(a, b, preferred_element_type=F32)


def dot_nt(a, b, precision=None):
    return lax.dot_general(
        a, b, (((1,), (1,)), ((), ())), precision=precision, preferred_element_type=F32
    )


def dot_tn(a, b, precision=None):
    return lax.dot_general(
        a, b, (((0,), (0,)), ((), ())), precision=precision, preferred_element_type=F32
    )


def normalize(values):
    center = values - jnp.mean(values, axis=-1, keepdims=True)
    rstd = lax.rsqrt(jnp.mean(center * center, axis=-1, keepdims=True) + EPS)
    return center * rstd, rstd


def norm_back(hat, rstd, gain, grad):
    inner = grad * gain
    mean = jnp.mean(inner, axis=-1, keepdims=True)
    along = jnp.mean(inner * hat, axis=-1, keepdims=True)
    return rstd * (inner - mean - hat * along)


def call(kernel, outs, ins, scratch=(), in_specs=None, out_specs=None, flops=0, vmem=8 * MIB, name=None):
    in_bytes = sum(x.size * x.dtype.itemsize for x in ins)
    return pl.pallas_call(
        kernel,
        out_shape=[jax.ShapeDtypeStruct(s, d) for s, d in outs],
        in_specs=in_specs or [VMEM] * len(ins),
        out_specs=out_specs or [VMEM] * len(outs),
        scratch_shapes=list(scratch),
        compiler_params=pltpu.CompilerParams(vmem_limit_bytes=vmem),
        cost_estimate=pl.CostEstimate(flops=flops, bytes_accessed=in_bytes, transcendentals=0),
        name=name,
    )(*ins)


def pick_kernel(seq, images, tok, cot, *refs):
    outs, sem = refs[:-1], refs[-1]
    me = lax.axis_index("seq")
    copies = []
    for k in range(seq):
        index = jnp.minimum(me ^ k, images - 1)
        for part, source in enumerate((tok, cot)):
            copies.append(
                pltpu.make_async_copy(source.at[index], outs[2 * k + part], sem.at[2 * k + part])
            )
    for copy in copies:
        copy.start()
    for copy in copies:
        copy.wait()


def prompt_kernel(prompts, gain, shift, w_qkv, b_qkv, w_out, w_up, w_down, out):
    count, width = prompts.shape
    rows = prompts[...].astype(BF16).astype(F32)
    hat, _ = normalize(rows)
    normed = (hat * gain[...] + shift[...]).astype(BF16)
    out[...] = jnp.zeros_like(out)
    for part in range(2):
        cols = pl.ds((part + 1) * width, width)
        here = dot(normed, w_qkv[:, cols]) + b_qkv[:, cols]
        out[:count, pl.ds(part * width, width)] = here.astype(BF16)


def main_kernel(
    seq,
    images,
    *refs,
):
    toks = refs[:seq]
    cots = refs[seq : 2 * seq]
    (
        mask,
        pkv,
        prompts,
        gain_one,
        shift_one,
        w_qkv,
        b_qkv,
        w_out,
        b_out,
        gain_two,
        shift_two,
        w_up,
        b_up,
        w_down,
        pgrad,
        act,
        resid,
        dres,
        p_bf,
        ds_bf,
        query,
        dmix,
        k_t,
        x,
        gbuf,
        tbuf,
        keys,
        values,
        v_t,
        mix_t,
        p_f,
        dhid,
        normed,
    ) = refs[2 * seq :]
    me = lax.axis_index("seq")
    chunk = toks[0].shape[0]
    rows, width = x.shape
    head = width // HEADS
    ff = act.shape[1]
    nkeys = keys.shape[0]
    count = prompts.shape[0]
    scale = head ** (-0.5)
    live = jnp.where(me < images, 1.0, 0.0)
    for k in range(seq):
        tbuf[k] = toks[k][...]
    for c in range(seq):
        x[pl.ds(c * chunk, chunk), :] = tbuf[me ^ c].astype(F32) * live
    for k in range(seq):
        tbuf[k] = cots[k][...]
    for c in range(seq):
        gbuf[pl.ds(c * chunk, chunk), :] = tbuf[me ^ c].astype(F32) * live

    hat, _ = normalize(x[...])
    normed[...] = (hat * gain_one[...] + shift_one[...]).astype(BF16)
    query[...] = (dot(normed[...], w_qkv[:, :width]) + b_qkv[:, :width]).astype(BF16)
    for part, dest in enumerate((keys, values)):
        cols = pl.ds((part + 1) * width, width)
        dest[:rows, :] = (dot(normed[...], w_qkv[:, cols]) + b_qkv[:, cols]).astype(BF16)
        dest[rows:, :] = pkv[: nkeys - rows, pl.ds(part * width, width)]
    k_t[...] = keys[...].T
    v_t[...] = values[...].T

    index = jnp.minimum(me, images - 1)
    mrow = mask[pl.ds(index, 1), :].astype(F32)
    mcol = dot_tn(
        jnp.broadcast_to(mrow, (8, rows)).astype(BF16), jnp.full((8, rows), 0.125, BF16)
    )
    bias_rows = jnp.where(mcol > 0.5, 0.0, -jnp.inf)
    rest = lax.broadcasted_iota(jnp.int32, (nkeys - rows, rows), 0)
    bias = jnp.concatenate([bias_rows, jnp.where(rest < count, 0.0, -jnp.inf)], 0)

    lane = lax.broadcasted_iota(jnp.int32, (rows, 2 * head), 1) // head
    for pair in range(HEADS // 2):
        cols = pl.ds(pair * 2 * head, 2 * head)
        qp = query[:, cols]
        kp = keys[:, cols]
        for side in range(2):
            h = pair * 2 + side
            qm = jnp.where(lane == side, qp, jnp.zeros_like(qp))
            score = dot_nt(kp, qm) * (scale * LOG2E) + bias
            top = jnp.max(score, axis=0, keepdims=True)
            ex = jnp.exp2(score - top)
            total = jnp.sum(ex, axis=0, keepdims=True)
            prob = ex * (1.0 / total)
            p_f[h] = prob
            weight = prob.astype(BF16)
            p_bf[h] = weight
            part = pl.ds(h * head, head)
            mix_t[part, :] = dot(v_t[part, :], weight).astype(BF16)

    resid[...] = x[...] + dot_tn(mix_t[...], w_out[...]) + b_out[...]
    hat_two, rstd_two = normalize(resid[...])
    normed[...] = (hat_two * gain_two[...] + shift_two[...]).astype(BF16)
    grad_out = gbuf[...].astype(BF16)
    step = 256

    def mlp(c, carry):
        cols = pl.ds(pl.multiple_of(c * step, step), step)
        hidden = dot(normed[...], w_up[:, cols]) + b_up[:, cols]
        grad = dot_nt(grad_out, w_down[cols, :])
        cdf = 0.5 * (1.0 + lax.erf(hidden * math.sqrt(0.5)))
        act[:, cols] = (hidden * cdf).astype(BF16)
        pdf = jnp.exp(-0.5 * hidden * hidden) * (1.0 / math.sqrt(2.0 * math.pi))
        dhid[:, cols] = (grad * (cdf + hidden * pdf)).astype(BF16)
        return carry

    lax.fori_loop(0, ff // step, mlp, 0)
    hat_two, rstd_two = normalize(resid[...])
    grad_resid = gbuf[...] + norm_back(
        hat_two, rstd_two, gain_two[...], dot_nt(dhid[...], w_up[...])
    )
    dres[...] = grad_resid
    dmix[...] = dot_nt(grad_resid.astype(BF16), w_out[...]).astype(BF16)

    gk = []
    gv = []
    for pair in range(HEADS // 2):
        cols = pl.ds(pair * 2 * head, 2 * head)
        qp = query[:, cols]
        gp = dmix[:, cols]
        vp = values[:, cols]
        gkp = jnp.zeros((nkeys - rows, 2 * head), F32)
        gvp = jnp.zeros((nkeys - rows, 2 * head), F32)
        for side in range(2):
            h = pair * 2 + side
            qm = jnp.where(lane == side, qp, jnp.zeros_like(qp))
            gm = jnp.where(lane == side, gp, jnp.zeros_like(gp))
            dprob = dot_nt(vp, gm)
            prob = p_f[h]
            both = prob * dprob
            inner = jnp.sum(both, axis=0, keepdims=True)
            draw = ((both - prob * inner) * scale).astype(BF16)
            ds_bf[h] = draw
            gkp = gkp + dot(draw[rows:, :], qm)
            gvp = gvp + dot(p_bf[h, rows:, :], gm)
        gk.append(gkp)
        gv.append(gvp)
    pad = pgrad.shape[0]
    grad_kv = jnp.concatenate(gk + gv, 1)[:pad, :]
    first = grad_kv.astype(BF16)
    left = grad_kv - first.astype(F32)
    second = left.astype(BF16)
    third = (left - second.astype(F32)).astype(BF16)
    w_kv = w_qkv[:, pl.ds(width, 2 * width)]
    three = dot_nt(jnp.concatenate([first, second, third], 0), w_kv)
    grad_normed = three[:pad] + three[pad : 2 * pad] + three[2 * pad :]
    prompt_rows = prompts[...].astype(BF16).astype(F32)
    hat_p, rstd_p = normalize(prompt_rows)
    pgrad[...] = jnp.zeros_like(pgrad)
    pgrad[:count, :] = norm_back(hat_p, rstd_p, gain_one[...], grad_normed[:count, :])


def send_out(me, seq, value, wide, cbuf, outs):
    chunk = outs[0].shape[0]
    wide[...] = value
    for c in range(seq):
        cbuf[c] = wide[pl.ds(c * chunk, chunk), :].astype(BF16)
    for k in range(seq):
        outs[k][...] = cbuf[me ^ k]


def down_kernel(seq, act, resid, w_down, b_down, *refs):
    outs, (wide, cbuf) = refs[:seq], refs[seq:]
    value = resid[...] + dot(act[...], w_down[...]) + b_down[...]
    send_out(lax.axis_index("seq"), seq, value, wide, cbuf, outs)


def attn_back_kernel(p_bf, ds_bf, query, dmix, k_t, dqkv, q_t):
    rows, width = query.shape
    head = width // HEADS
    lane = lax.broadcasted_iota(jnp.int32, (rows, 2 * head), 1) // head
    for pair in range(HEADS // 2):
        cols = pl.ds(pair * 2 * head, 2 * head)
        qp = query[:, cols]
        gp = dmix[:, cols]
        gk = jnp.zeros((rows, 2 * head), F32)
        gv = jnp.zeros((rows, 2 * head), F32)
        for side in range(2):
            h = pair * 2 + side
            part = pl.ds(h * head, head)
            q_t[part, :] = dot(k_t[part, :], ds_bf[h]).astype(BF16)
            gk = gk + dot(ds_bf[h, :rows, :], jnp.where(lane == side, qp, jnp.zeros_like(qp)))
            gv = gv + dot(p_bf[h, :rows, :], jnp.where(lane == side, gp, jnp.zeros_like(gp)))
        dqkv[:, pl.ds(width + pair * 2 * head, 2 * head)] = gk.astype(BF16)
        dqkv[:, pl.ds(2 * width + pair * 2 * head, 2 * head)] = gv.astype(BF16)
    dqkv[:, :width] = q_t[...].T


def input_kernel(seq, dqkv, w_qkv, x, dres, gain, *refs):
    outs, (wide, cbuf) = refs[:seq], refs[seq:]
    hat, rstd = normalize(x[...])
    value = dres[...] + norm_back(hat, rstd, gain[...], dot_nt(dqkv[...], w_qkv[...]))
    send_out(lax.axis_index("seq"), seq, value, wide, cbuf, outs)


def place_kernel(seq, images, *refs):
    ins, (out, sem) = refs[:seq], refs[seq:]
    me = lax.axis_index("seq")

    def copy(k):
        return pltpu.make_async_copy(ins[k], out.at[me ^ k], sem.at[k])

    for k in range(seq):
        @pl.when((me ^ k) < images)
        def _():
            copy(k).start()

    for k in range(seq):
        @pl.when((me ^ k) < images)
        def _():
            copy(k).wait()


def final_kernel(
    total, mine, other, combined, start_t, prompts, momentum,
    basis_t, right_t, error, new_momentum, new_prompts, prompt_copy, whole,
):
    half = mine.shape[1]
    count, width = prompts.shape
    rank = start_t.shape[0]
    core = lax.rem(lax.axis_index("dp"), 2)
    whole[:, :half] = jnp.where(core == 0, mine[...], other[...])
    whole[:, half:] = jnp.where(core == 0, other[...], mine[...])
    summed = whole[...]
    left = dot_nt(start_t[...], summed, HIGHEST)
    row = lax.broadcasted_iota(jnp.int32, left.shape, 0)
    for j in range(rank):
        pivot = left[j : j + 1, :]
        pivot = pivot * lax.rsqrt(jnp.sum(pivot * pivot, axis=1, keepdims=True) + 1e-12)
        along = jnp.sum(left * pivot, axis=1, keepdims=True)
        left = jnp.where(row > j, left - along * pivot, jnp.where(row == j, pivot, left))
    right = jnp.dot(left, summed, precision=HIGHEST, preferred_element_type=F32)
    mine_w = combined[...]
    right_w = jnp.dot(left, mine_w, precision=HIGHEST, preferred_element_type=F32)
    error[:, 0, :] = (mine_w - dot_tn(left, right_w, HIGHEST))[:count, :]
    update = dot_tn(left, right, HIGHEST)[:count, :] / total
    moved = MOMENTUM_DECAY * momentum[...] + update
    fresh = prompts[...] - RATE_SCALE * math.sqrt(total) * moved
    basis_t[...] = left[:, :count]
    right_t[...] = right
    new_momentum[...] = moved
    new_prompts[...] = fresh
    prompt_copy[...] = fresh.astype(BF16)


def flip(k, n):
    return [(i, i ^ k) for i in range(n)]


def body(
    tokens,
    key_mask,
    prompts,
    gain_one,
    shift_one,
    w_qkv,
    b_qkv,
    w_out,
    b_out,
    gain_two,
    shift_two,
    w_up,
    b_up,
    w_down,
    b_down,
    cotangent,
    start_factor,
    error_buffer,
    momentum,
):
    images, chunk, width = tokens.shape
    seq = lax.axis_size("seq")
    dp = lax.axis_size("dp")
    rows = seq * chunk
    ff = w_up.shape[1]
    count = prompts.shape[0]
    if images > seq or seq & (seq - 1) or dp & (dp - 1):
        raise ValueError("unsupported mesh")
    nkeys = up(rows + count, 16)
    pad = up(count, 8)
    gain_one, shift_one, b_qkv, b_out, gain_two, shift_two, b_up, b_down = (
        v.reshape(1, -1)
        for v in (gain_one, shift_one, b_qkv, b_out, gain_two, shift_two, b_up, b_down)
    )

    piece = ((chunk, width), BF16)
    picked = call(
        functools.partial(pick_kernel, seq, images),
        [piece] * (2 * seq),
        (tokens, cotangent),
        [pltpu.SemaphoreType.DMA((2 * seq,))],
        in_specs=[ANY] * 2,
        name="pick",
    )
    toks, cots = [picked[0]], [picked[1]]
    for k in range(1, seq):
        pairs = [(a, b) for a, b in flip(k, seq) if b < images]
        toks.append(lax.ppermute(picked[2 * k], "seq", pairs))
    for k in range(1, seq):
        pairs = [(a, b) for a, b in flip(k, seq) if b < images]
        cots.append(lax.ppermute(picked[2 * k + 1], "seq", pairs))

    (pkv,) = call(
        prompt_kernel,
        [((up(count, 16), 2 * width), BF16)],
        (prompts, gain_one, shift_one, w_qkv, b_qkv, w_out, w_up, w_down),
        flops=2 * count * width * 2 * width,
        name="prompt_kv",
    )

    outs = [
        ((pad, width), F32),
        ((rows, ff), BF16),
        ((rows, width), F32),
        ((rows, width), F32),
        ((HEADS, nkeys, rows), BF16),
        ((HEADS, nkeys, rows), BF16),
        ((rows, width), BF16),
        ((rows, width), BF16),
        ((width, nkeys), BF16),
        ((rows, width), F32),
    ]
    pgrad, act, resid, dres, p_bf, ds_bf, query, dmix, k_t, x = call(
        functools.partial(main_kernel, seq, images),
        outs,
        (
            *toks, *cots, key_mask, pkv, prompts, gain_one, shift_one, w_qkv, b_qkv, w_out, b_out,
            gain_two, shift_two, w_up, b_up, w_down,
        ),
        [
            pltpu.VMEM((rows, width), F32),
            pltpu.VMEM((seq, chunk, width), BF16),
            pltpu.VMEM((nkeys, width), BF16),
            pltpu.VMEM((nkeys, width), BF16),
            pltpu.VMEM((width, nkeys), BF16),
            pltpu.VMEM((width, rows), BF16),
            pltpu.VMEM((HEADS, nkeys, rows), F32),
            pltpu.VMEM((rows, ff), BF16),
            pltpu.VMEM((rows, width), BF16),
        ],
        flops=2 * rows * width * (4 * width + 3 * ff),
        vmem=24 * MIB,
        name="layer",
    )

    combined = pgrad
    for k in range(1, seq):
        combined = combined + lax.ppermute(pgrad, "seq", flip(k, seq))
    padded_error = jnp.pad(error_buffer[0], ((0, pad - count), (0, 0)))
    combined = combined + padded_error
    half = width // 2
    core = lax.rem(lax.axis_index("dp"), 2)
    keep = lax.dynamic_slice(combined, (0, core * half), (pad, half))
    give = lax.dynamic_slice(combined, (0, (1 - core) * half), (pad, half))
    mine = keep + lax.ppermute(give, "dp", flip(1, dp))
    bit = 2
    while bit < dp:
        steps = [bit, 2 * bit, 3 * bit] if 2 * bit < dp else [bit]
        mine = mine + sum(lax.ppermute(mine, "dp", flip(k, dp)) for k in steps)
        bit *= 4 if 2 * bit < dp else 2
    other = lax.ppermute(mine, "dp", flip(1, dp))

    low_chunks = call(
        functools.partial(down_kernel, seq),
        [piece] * seq,
        (act, resid, w_down, b_down),
        [pltpu.VMEM((rows, width), F32), pltpu.VMEM((seq, chunk, width), BF16)],
        flops=2 * rows * width * ff,
        name="down",
    )
    (dqkv,) = call(
        attn_back_kernel,
        [((rows, 3 * width), BF16)],
        (p_bf, ds_bf, query, dmix, k_t),
        [pltpu.VMEM((width, rows), BF16)],
        flops=6 * rows * width * nkeys,
        name="attn_back",
    )
    grad_chunks = call(
        functools.partial(input_kernel, seq),
        [piece] * seq,
        (dqkv, w_qkv, x, dres, gain_one),
        [pltpu.VMEM((rows, width), F32), pltpu.VMEM((seq, chunk, width), BF16)],
        flops=6 * rows * width * width,
        name="input_grad",
    )
    results = []
    for chunks in (low_chunks, grad_chunks):
        back = [chunks[0]]
        for k in range(1, seq):
            pairs = [(a, b) for a, b in flip(k, seq) if a < images]
            back.append(lax.ppermute(chunks[k], "seq", pairs))
        (placed,) = call(
            functools.partial(place_kernel, seq, images),
            [((images, chunk, width), BF16)],
            back,
            [pltpu.SemaphoreType.DMA((seq,))],
            in_specs=[ANY] * seq,
            out_specs=[ANY],
            name="place",
        )
        results.append(placed)
    layer_out, input_grad = results

    rank = start_factor.shape[1]
    basis_t, right_t, error, new_momentum, new_prompts, prompt_copy = call(
        functools.partial(final_kernel, images * dp),
        [
            ((rank, count), F32),
            ((rank, width), F32),
            ((count, 1, width), F32),
            ((count, width), F32),
            ((count, width), F32),
            ((count, width), BF16),
        ],
        (mine, other, combined, start_factor.T, prompts, momentum),
        [pltpu.VMEM((pad, width), F32)],
        name="final",
    )
    return (
        layer_out,
        input_grad,
        basis_t.T,
        right_t.T,
        error.transpose(1, 0, 2),
        new_momentum,
        new_prompts,
        prompt_copy,
    )


def solution(mesh):
    rep = P()
    rows = P("dp", "seq", None)
    placed = (rows, P("dp", None), *([rep] * 13), rows, rep, P("dp", None, None), rep)
    return jax.shard_map(
        body,
        mesh=mesh,
        in_specs=placed,
        out_specs=(rows, rows, rep, rep, P("dp", None, None), rep, rep, rep),
        check_vma=False,
    )
```

```python
import functools
import math

import jax
import jax.numpy as jnp
from jax import lax
from jax.experimental import pallas as pl
from jax.experimental.pallas import tpu as pltpu
from jax.sharding import PartitionSpec as P

HEADS = 12
EPS = 1e-06
MOMENTUM_DECAY = 0.5
RATE_SCALE = 3.0
HIGHEST = lax.Precision.HIGHEST
F32 = jnp.float32
BF16 = jnp.bfloat16
VMEM = pl.BlockSpec(memory_space=pltpu.VMEM)
ANY = pl.BlockSpec(memory_space=pl.ANY)
HBM = pl.BlockSpec(memory_space=pltpu.HBM)
MIB = 1 << 20
LOG2E = 1.4426950408889634


def up(value, unit):
    return -(-value // unit) * unit


def dot(a, b):
    return jnp.dot(a, b, preferred_element_type=F32)


def dot_nt(a, b, precision=None):
    return lax.dot_general(
        a, b, (((1,), (1,)), ((), ())), precision=precision, preferred_element_type=F32
    )


def dot_tn(a, b, precision=None):
    return lax.dot_general(
        a, b, (((0,), (0,)), ((), ())), precision=precision, preferred_element_type=F32
    )


def normalize(values):
    center = values - jnp.mean(values, axis=-1, keepdims=True)
    rstd = lax.rsqrt(jnp.mean(center * center, axis=-1, keepdims=True) + EPS)
    return center * rstd, rstd


def norm_back(hat, rstd, gain, grad):
    inner = grad * gain
    mean = jnp.mean(inner, axis=-1, keepdims=True)
    along = jnp.mean(inner * hat, axis=-1, keepdims=True)
    return rstd * (inner - mean - hat * along)


def call(kernel, outs, ins, scratch=(), in_specs=None, out_specs=None, flops=0, vmem=8 * MIB, name=None):
    in_specs = in_specs or [VMEM] * len(ins)
    out_specs = out_specs or [VMEM] * len(outs)
    ins = [
        pltpu.with_memory_space_constraint(x, pltpu.HBM) if spec is HBM else x
        for x, spec in zip(ins, in_specs)
    ]
    held = {id(VMEM): pltpu.VMEM, id(HBM): pltpu.HBM}
    return pl.pallas_call(
        kernel,
        out_shape=[
            held.get(id(spec), jax.ShapeDtypeStruct)(s, d) for (s, d), spec in zip(outs, out_specs)
        ],
        in_specs=in_specs,
        out_specs=out_specs,
        scratch_shapes=list(scratch),
        compiler_params=pltpu.CompilerParams(vmem_limit_bytes=vmem),
        cost_estimate=pl.CostEstimate(
            flops=flops,
            bytes_accessed=sum(x.size * x.dtype.itemsize for x in ins),
            transcendentals=0,
        ),
        name=name,
    )(*ins)


class Copies:
    def __init__(self, sems):
        self.sems = sems
        self.used = 0

    def __call__(self, source, target):
        copy = pltpu.make_async_copy(source, target, self.sems.at[self.used])
        self.used += 1
        copy.start()
        return copy


def wait(*copies):
    for copy in copies:
        copy.wait()


def pick_kernel(seq, images, tok, cot, *refs):
    outs, sems = refs[:-1], refs[-1]
    me = lax.axis_index("seq")
    start = Copies(sems)
    copies = []
    for k in range(seq):
        index = jnp.minimum(me ^ k, images - 1)
        copies.append(start(tok.at[index], outs[k].at[0]))
        copies.append(start(cot.at[index], outs[k].at[1]))
    wait(*copies)


def prepare_kernel(count_in, *refs):
    sources, targets = refs[:count_in], refs[count_in : 2 * count_in]
    pkv, sems = refs[2 * count_in :]
    start = Copies(sems)
    copies = [
        start(a, b if len(a.shape) == len(b.shape) else b.at[0]) for a, b in zip(sources, targets)
    ]
    prompts, gain, shift, b_qkv, w_qkv = targets[:5]
    count, width = prompts.shape
    cols = pl.ds(width, 2 * width)
    pkv[...] = jnp.zeros_like(pkv)
    wait(*copies[:4])
    hat, _ = normalize(prompts[...].astype(BF16).astype(F32))
    normed = (hat * gain[...] + shift[...]).astype(BF16)
    wait(copies[4])
    pkv[:count, :] = (dot(normed, w_qkv[:, cols]) + b_qkv[:, cols]).astype(BF16)
    wait(*copies[5:])


def layer_kernel(seq, images, *refs):
    packs = refs[:seq]
    (
        mask, pkv, prompts, gain_one, shift_one, b_qkv, w_qkv, w_out, b_out, gain_two, shift_two,
        w_up, b_up, w_down, error,
        pgrad, base, act, resid, dres, p_bf, ds_bf, query, dmix, k_t, x_bf,
        x, gbuf, tbuf, keys, values, v_t, mix_t, p_f, dhid, normed,
    ) = refs[seq:]
    me = lax.axis_index("seq")
    chunk = packs[0].shape[1]
    rows, width = x.shape
    head = width // HEADS
    ff = act.shape[1]
    nkeys = keys.shape[0]
    count = prompts.shape[0]
    scale = head ** (-0.5)
    parts = [pl.ds(part * width, width) for part in range(3)]

    live = jnp.where(me < images, 1.0, 0.0)
    for k in range(seq):
        tbuf[k] = packs[k][...]
    for c in range(seq):
        span = pl.ds(c * chunk, chunk)
        x[span, :] = tbuf[me ^ c, 0].astype(F32) * live
        gbuf[span, :] = tbuf[me ^ c, 1].astype(F32) * live
    x_bf[...] = x[...].astype(BF16)
    hat, _ = normalize(x[...])
    normed[...] = (hat * gain_one[...] + shift_one[...]).astype(BF16)
    query[...] = (dot(normed[...], w_qkv[:, parts[0]]) + b_qkv[:, parts[0]]).astype(BF16)
    for index, dest in ((1, keys), (2, values)):
        part = parts[index]
        dest[:rows, :] = (dot(normed[...], w_qkv[:, part]) + b_qkv[:, part]).astype(BF16)
        dest[rows:, :] = pkv[: nkeys - rows, parts[index - 1]]
    k_t[...] = keys[...].T
    v_t[...] = values[...].T

    mrow = mask[pl.ds(jnp.minimum(me, images - 1), 1), :].astype(F32)
    mcol = dot_tn(
        jnp.broadcast_to(mrow, (8, rows)).astype(BF16), jnp.full((8, rows), 0.125, BF16)
    )
    rest = lax.broadcasted_iota(jnp.int32, (nkeys - rows, rows), 0)
    bias = jnp.concatenate(
        [jnp.where(mcol > 0.5, 0.0, -jnp.inf), jnp.where(rest < count, 0.0, -jnp.inf)], 0
    )

    lane = lax.broadcasted_iota(jnp.int32, (rows, 2 * head), 1) // head
    for pair in range(HEADS // 2):
        cols = pl.ds(pair * 2 * head, 2 * head)
        qp = query[:, cols]
        kp = keys[:, cols]
        for side in range(2):
            h = pair * 2 + side
            qm = jnp.where(lane == side, qp, jnp.zeros_like(qp))
            score = dot_nt(kp, qm) * (scale * LOG2E) + bias
            top = jnp.max(score, axis=0, keepdims=True)
            ex = jnp.exp2(score - top)
            total = jnp.sum(ex, axis=0, keepdims=True)
            prob = ex * (1.0 / total)
            p_f[h] = prob
            weight = prob.astype(BF16)
            p_bf[h] = weight
            part = pl.ds(h * head, head)
            mix_t[part, :] = dot(v_t[part, :], weight).astype(BF16)

    resid[...] = x[...] + dot_tn(mix_t[...], w_out[...]) + b_out[...]
    hat_two, _ = normalize(resid[...])
    normed[...] = (hat_two * gain_two[...] + shift_two[...]).astype(BF16)
    grad_out = gbuf[...].astype(BF16)
    step = 256

    def mlp(c, carry):
        cols = pl.ds(pl.multiple_of(c * step, step), step)
        hidden = dot(normed[...], w_up[:, cols]) + b_up[:, cols]
        grad = dot_nt(grad_out, w_down[cols, :])
        cdf = 0.5 * (1.0 + lax.erf(hidden * math.sqrt(0.5)))
        act[:, cols] = (hidden * cdf).astype(BF16)
        pdf = jnp.exp(-0.5 * hidden * hidden) * (1.0 / math.sqrt(2.0 * math.pi))
        dhid[:, cols] = (grad * (cdf + hidden * pdf)).astype(BF16)
        return carry

    lax.fori_loop(0, ff // step, mlp, 0)
    hat_two, rstd_two = normalize(resid[...])
    grad_resid = gbuf[...] + norm_back(
        hat_two, rstd_two, gain_two[...], dot_nt(dhid[...], w_up[...])
    )
    dres[...] = grad_resid
    dmix[...] = dot_nt(grad_resid.astype(BF16), w_out[...]).astype(BF16)

    gk = []
    gv = []
    for pair in range(HEADS // 2):
        cols = pl.ds(pair * 2 * head, 2 * head)
        qp = query[:, cols]
        gp = dmix[:, cols]
        vp = values[:, cols]
        gkp = jnp.zeros((nkeys - rows, 2 * head), F32)
        gvp = jnp.zeros((nkeys - rows, 2 * head), F32)
        for side in range(2):
            h = pair * 2 + side
            qm = jnp.where(lane == side, qp, jnp.zeros_like(qp))
            gm = jnp.where(lane == side, gp, jnp.zeros_like(gp))
            dprob = dot_nt(vp, gm)
            prob = p_f[h]
            both = prob * dprob
            inner = jnp.sum(both, axis=0, keepdims=True)
            draw = ((both - prob * inner) * scale).astype(BF16)
            ds_bf[h] = draw
            gkp = gkp + dot(draw[rows:, :], qm)
            gvp = gvp + dot(p_bf[h, rows:, :], gm)
        gk.append(gkp)
        gv.append(gvp)
    pad = pgrad.shape[0]
    grad_kv = jnp.concatenate(gk + gv, 1)[:pad, :]
    first = grad_kv.astype(BF16)
    left = grad_kv - first.astype(F32)
    second = left.astype(BF16)
    third = (left - second.astype(F32)).astype(BF16)
    w_kv = w_qkv[:, pl.ds(width, 2 * width)]
    three = dot_nt(jnp.concatenate([first, second, third], 0), w_kv)
    grad_normed = three[:pad] + three[pad : 2 * pad] + three[2 * pad :]
    hat_p, rstd_p = normalize(prompts[...].astype(BF16).astype(F32))
    part = norm_back(hat_p, rstd_p, gain_one[...], grad_normed[:count, :]).astype(pgrad.dtype)
    pgrad[...] = jnp.zeros_like(pgrad)
    pgrad[:count, :] = part
    base[...] = jnp.zeros_like(base)
    base[:count, :] = error[:, 0, :]


def rest_kernel(
    seq, act, resid, dres, p_bf, ds_bf, query, dmix, k_t, x_bf, w_down, w_qkv, b_down, gain,
    out, grad, dqkv, q_t, wide,
):
    rows, width = query.shape
    head = width // HEADS
    chunk = out.shape[1]
    lane = lax.broadcasted_iota(jnp.int32, (rows, 2 * head), 1) // head
    for pair in range(HEADS // 2):
        cols = pl.ds(pair * 2 * head, 2 * head)
        qp = query[:, cols]
        gp = dmix[:, cols]
        gk = jnp.zeros((rows, 2 * head), F32)
        gv = jnp.zeros((rows, 2 * head), F32)
        for side in range(2):
            h = pair * 2 + side
            part = pl.ds(h * head, head)
            q_t[part, :] = dot(k_t[part, :], ds_bf[h]).astype(BF16)
            gk = gk + dot(ds_bf[h, :rows, :], jnp.where(lane == side, qp, jnp.zeros_like(qp)))
            gv = gv + dot(p_bf[h, :rows, :], jnp.where(lane == side, gp, jnp.zeros_like(gp)))
        dqkv[:, pl.ds(width + pair * 2 * head, 2 * head)] = gk.astype(BF16)
        dqkv[:, pl.ds(2 * width + pair * 2 * head, 2 * head)] = gv.astype(BF16)
    dqkv[:, :width] = q_t[...].T
    wide[...] = resid[...] + dot(act[...], w_down[...]) + b_down[...]
    for c in range(seq):
        out[c] = wide[pl.ds(c * chunk, chunk), :].astype(BF16)
    hat, rstd = normalize(x_bf[...].astype(F32))
    wide[...] = dres[...] + norm_back(hat, rstd, gain[...], dot_nt(dqkv[...], w_qkv[...]))
    for c in range(seq):
        grad[c] = wide[pl.ds(c * chunk, chunk), :].astype(BF16)


def pack_kernel(seq, out, grad, after, *packs):
    me = lax.axis_index("seq")
    for k in range(seq):
        packs[k][0] = out[me ^ k]
        packs[k][1] = grad[me ^ k]


def place_kernel(seq, images, *refs):
    ins, (out, grad, sems) = refs[:seq], refs[seq:]
    me = lax.axis_index("seq")

    def copies(k):
        return (
            pltpu.make_async_copy(ins[k].at[0], out.at[me ^ k], sems.at[2 * k]),
            pltpu.make_async_copy(ins[k].at[1], grad.at[me ^ k], sems.at[2 * k + 1]),
        )

    for k in range(seq):
        @pl.when((me ^ k) < images)
        def _():
            for copy in copies(k):
                copy.start()

    for k in range(seq):
        @pl.when((me ^ k) < images)
        def _():
            for copy in copies(k):
                copy.wait()


def tree(values):
    while len(values) > 1:
        values = [
            values[i] + values[i + 1] if i + 1 < len(values) else values[i]
            for i in range(0, len(values), 2)
        ]
    return values[0]


def combine_kernel(*refs):
    base, parts, (combined, keep, give) = refs[0], refs[1:-4], refs[-3:]
    half = keep.shape[1]
    core = lax.rem(lax.axis_index("dp"), 2)
    combined[...] = tree([part[...].astype(F32) for part in parts]) + base[...]
    low, high = combined[:, :half], combined[:, half:]
    keep[...] = jnp.where(core == 0, low, high)
    give[...] = jnp.where(core == 0, high, low)


def add_kernel(*refs):
    parts, out = refs[:-1], refs[-1]
    out[...] = tree([part[...].astype(F32) for part in parts]).astype(out.dtype)


def final_kernel(
    total, mine, other, combined, start_t, prompts, momentum,
    basis_t, right_t, error, new_momentum, new_prompts, prompt_copy, whole,
):
    half = mine.shape[1]
    count, width = prompts.shape
    rank = start_t.shape[0]
    core = lax.rem(lax.axis_index("dp"), 2)
    whole[:, :half] = jnp.where(core == 0, mine[...], other[...])
    whole[:, half:] = jnp.where(core == 0, other[...], mine[...])
    summed = whole[...]
    left = dot_nt(start_t[...], summed, HIGHEST)
    row = lax.broadcasted_iota(jnp.int32, left.shape, 0)
    for j in range(rank):
        pivot = left[j : j + 1, :]
        pivot = pivot * lax.rsqrt(jnp.sum(pivot * pivot, axis=1, keepdims=True) + 1e-12)
        along = jnp.sum(left * pivot, axis=1, keepdims=True)
        left = jnp.where(row > j, left - along * pivot, jnp.where(row == j, pivot, left))
    right = jnp.dot(left, summed, precision=HIGHEST, preferred_element_type=F32)
    mine_w = combined[...]
    right_w = jnp.dot(left, mine_w, precision=HIGHEST, preferred_element_type=F32)
    error[:, 0, :] = (mine_w - dot_tn(left, right_w, HIGHEST))[:count, :]
    update = dot_tn(left, right, HIGHEST)[:count, :] / total
    moved = MOMENTUM_DECAY * momentum[...] + update
    fresh = prompts[...] - RATE_SCALE * math.sqrt(total) * moved
    basis_t[...] = left[:, :count]
    right_t[...] = right
    new_momentum[...] = moved
    new_prompts[...] = fresh
    prompt_copy[...] = fresh.astype(BF16)


def flip(k, n):
    return [(i, i ^ k) for i in range(n)]


def body(
    tokens,
    key_mask,
    prompts,
    gain_one,
    shift_one,
    w_qkv,
    b_qkv,
    w_out,
    b_out,
    gain_two,
    shift_two,
    w_up,
    b_up,
    w_down,
    b_down,
    cotangent,
    start_factor,
    error_buffer,
    momentum,
):
    images, chunk, width = tokens.shape
    seq = lax.axis_size("seq")
    dp = lax.axis_size("dp")
    rows = seq * chunk
    ff = w_up.shape[1]
    count = prompts.shape[0]
    if images > seq or seq & (seq - 1) or dp & (dp - 1):
        raise ValueError("unsupported mesh")
    nkeys = up(rows + count, 16)
    pad = up(count, 8)
    dma = pltpu.SemaphoreType.DMA

    piece = ((2, chunk, width), BF16)
    packs = call(
        functools.partial(pick_kernel, seq, images),
        [piece] * seq,
        (tokens, cotangent),
        [dma((2 * seq,))],
        in_specs=[HBM] * 2,
        name="pick",
    )
    packs = [packs[0]] + [
        lax.ppermute(packs[k], "seq", flip(k, seq)) for k in range(1, seq)
    ]

    loads = (
        prompts, gain_one, shift_one, b_qkv, w_qkv, w_out, b_out, gain_two, shift_two, w_up, b_up,
        w_down, error_buffer.transpose(1, 0, 2), b_down,
    )
    *held, pkv = call(
        functools.partial(prepare_kernel, len(loads)),
        [((1, v.size) if v.ndim == 1 else v.shape, v.dtype) for v in loads]
        + [((up(count, 16), 2 * width), BF16)],
        loads,
        [dma((len(loads),))],
        in_specs=[HBM] * len(loads),
        flops=2 * count * width * 2 * width,
        name="prepare",
    )
    held, b_down_row = held[:-1], held[-1]
    gain_row, w_qkv_held, w_down_held = held[1], held[4], held[11]

    wire = BF16
    saved = [
        ((rows, ff), BF16),
        ((rows, width), F32),
        ((rows, width), F32),
        ((HEADS, nkeys, rows), BF16),
        ((HEADS, nkeys, rows), BF16),
        ((rows, width), BF16),
        ((rows, width), BF16),
        ((width, nkeys), BF16),
        ((rows, width), BF16),
    ]
    pgrad, base, *kept = call(
        functools.partial(layer_kernel, seq, images),
        [((pad, width), wire), ((pad, width), F32)] + saved,
        (*packs, key_mask, pkv, *held),
        [
            pltpu.VMEM((rows, width), F32),
            pltpu.VMEM((rows, width), F32),
            pltpu.VMEM((seq, 2, chunk, width), BF16),
            pltpu.VMEM((nkeys, width), BF16),
            pltpu.VMEM((nkeys, width), BF16),
            pltpu.VMEM((width, nkeys), BF16),
            pltpu.VMEM((width, rows), BF16),
            pltpu.VMEM((HEADS, nkeys, rows), F32),
            pltpu.VMEM((rows, ff), BF16),
            pltpu.VMEM((rows, width), BF16),
        ],
        flops=2 * rows * width * (4 * width + 3 * ff),
        vmem=20 * MIB,
        name="layer",
    )

    out_chunks, grad_chunks = call(
        functools.partial(rest_kernel, seq),
        [((seq, chunk, width), BF16)] * 2,
        (*kept, w_down_held, w_qkv_held, b_down_row, gain_row),
        [
            pltpu.VMEM((rows, 3 * width), BF16),
            pltpu.VMEM((width, rows), BF16),
            pltpu.VMEM((rows, width), F32),
        ],
        flops=2 * rows * width * (3 * width + ff),
        vmem=8 * MIB,
        name="rest",
    )

    parts = [pgrad] + [lax.ppermute(pgrad, "seq", flip(k, seq)) for k in range(1, seq)]
    half = width // 2
    combined, keep, give = call(
        combine_kernel,
        [((pad, width), F32), ((pad, half), F32), ((pad, half), F32)],
        (base, *parts, out_chunks),
        in_specs=[VMEM] * (1 + seq) + [ANY],
        name="combine",
    )
    parts = [keep, lax.ppermute(give, "dp", flip(1, dp))]
    bit = 2
    first = None
    while bit < dp:
        (mine,) = call(add_kernel, [((pad, half), F32)], parts, name="add")
        first = mine if first is None else first
        steps = [bit, 2 * bit, 3 * bit] if 2 * bit < dp else [bit]
        parts = [mine] + [lax.ppermute(mine, "dp", flip(k, dp)) for k in steps]
        bit *= 4 if 2 * bit < dp else 2
    (mine,) = call(add_kernel, [((pad, half), F32)], parts, name="add")
    other = lax.ppermute(mine, "dp", flip(1, dp))

    packs = call(
        functools.partial(pack_kernel, seq),
        [piece] * seq,
        (out_chunks, grad_chunks, first),
        in_specs=[VMEM] * 2 + [ANY],
        name="pack",
    )
    back = [packs[0]] + [
        lax.ppermute(packs[k], "seq", flip(k, seq)) for k in range(1, seq)
    ]
    layer_out, input_grad = call(
        functools.partial(place_kernel, seq, images),
        [((images, chunk, width), BF16)] * 2,
        back,
        [dma((2 * seq,))],
        in_specs=[ANY] * seq,
        out_specs=[ANY] * 2,
        name="place",
    )

    rank = start_factor.shape[1]
    basis_t, right_t, error, new_momentum, new_prompts, prompt_copy = call(
        functools.partial(final_kernel, images * dp),
        [
            ((rank, count), F32),
            ((rank, width), F32),
            ((count, 1, width), F32),
            ((count, width), F32),
            ((count, width), F32),
            ((count, width), BF16),
        ],
        (mine, other, combined, start_factor.T, prompts, momentum),
        [pltpu.VMEM((pad, width), F32)],
        out_specs=[pl.BlockSpec(memory_space=pltpu.VMEM) for _ in range(6)],
        name="final",
    )
    return (
        layer_out,
        input_grad,
        basis_t.T,
        right_t.T,
        error.transpose(1, 0, 2),
        new_momentum,
        new_prompts,
        prompt_copy,
    )


def solution(mesh):
    rep = P()
    rows = P("dp", "seq", None)
    placed = (rows, P("dp", None), *([rep] * 13), rows, rep, P("dp", None, None), rep)
    return jax.shard_map(
        body,
        mesh=mesh,
        in_specs=placed,
        out_specs=(rows, rows, rep, rep, P("dp", None, None), rep, rep, rep),
        check_vma=False,
    )
```

```python
import functools
import math

import jax
import jax.numpy as jnp
from jax import lax
from jax.experimental import pallas as pl
from jax.experimental.pallas import tpu as pltpu
from jax.sharding import PartitionSpec as P

HEADS = 12
EPS = 1e-06
MOMENTUM_DECAY = 0.5
RATE_SCALE = 3.0
HIGH = lax.Precision.HIGH
F32 = jnp.float32
BF16 = jnp.bfloat16
VMEM = pl.BlockSpec(memory_space=pltpu.VMEM)
ANY = pl.BlockSpec(memory_space=pl.ANY)
HBM = pl.BlockSpec(memory_space=pltpu.HBM)
MIB = 1 << 20
LOG2E = 1.4426950408889634


def up(value, unit):
    return -(-value // unit) * unit


def dot(a, b):
    return jnp.dot(a, b, preferred_element_type=F32)


def dot_nt(a, b, precision=None):
    return lax.dot_general(
        a, b, (((1,), (1,)), ((), ())), precision=precision, preferred_element_type=F32
    )


def dot_tn(a, b, precision=None):
    return lax.dot_general(
        a, b, (((0,), (0,)), ((), ())), precision=precision, preferred_element_type=F32
    )


def normalize(values):
    center = values - jnp.mean(values, axis=-1, keepdims=True)
    rstd = lax.rsqrt(jnp.mean(center * center, axis=-1, keepdims=True) + EPS)
    return center * rstd, rstd


def norm_back(hat, rstd, gain, grad):
    inner = grad * gain
    mean = jnp.mean(inner, axis=-1, keepdims=True)
    along = jnp.mean(inner * hat, axis=-1, keepdims=True)
    return rstd * (inner - mean - hat * along)


def call(kernel, outs, ins, scratch=(), in_specs=None, out_specs=None, flops=0, vmem=8 * MIB, name=None):
    in_specs = in_specs or [VMEM] * len(ins)
    out_specs = out_specs or [VMEM] * len(outs)
    ins = [
        pltpu.with_memory_space_constraint(x, pltpu.HBM) if spec is HBM else x
        for x, spec in zip(ins, in_specs)
    ]
    held = {id(VMEM): pltpu.VMEM, id(HBM): pltpu.HBM}
    return pl.pallas_call(
        kernel,
        out_shape=[
            held.get(id(spec), jax.ShapeDtypeStruct)(s, d) for (s, d), spec in zip(outs, out_specs)
        ],
        in_specs=in_specs,
        out_specs=out_specs,
        scratch_shapes=list(scratch),
        compiler_params=pltpu.CompilerParams(vmem_limit_bytes=vmem),
        cost_estimate=pl.CostEstimate(
            flops=flops,
            bytes_accessed=sum(x.size * x.dtype.itemsize for x in ins),
            transcendentals=0,
        ),
        name=name,
    )(*ins)


class Copies:
    def __init__(self, sems):
        self.sems = sems
        self.used = 0

    def __call__(self, source, target):
        copy = pltpu.make_async_copy(source, target, self.sems.at[self.used])
        self.used += 1
        copy.start()
        return copy


def wait(*copies):
    for copy in copies:
        copy.wait()


def pick_kernel(seq, images, small, source, *refs):
    sources, refs = refs[:small], refs[small:]
    chunks, targets, sems = refs[:seq], refs[seq:-1], refs[-1]
    me = lax.axis_index("seq")
    start = Copies(sems)
    copies = [
        start(source.at[jnp.minimum(me ^ k, images - 1)], chunks[k]) for k in range(seq)
    ]
    for a, b in zip(sources, targets):
        copies.append(start(a, b if len(a.shape) > 1 else b.at[0]))
    wait(*copies)


def forward_kernel(seq, images, *refs):
    toks, refs = refs[:seq], refs[seq:]
    (
        mask, prompts, gain_one, shift_one, b_qkv, b_out, gain_two, shift_two, w_qkv, w_out,
        x_bf, query, keys, values, p_f, p_bf, resid, normed_two,
        x, tbuf, normed, bias, mix_t,
    ) = refs
    me = lax.axis_index("seq")
    rows, width = x.shape
    chunk = rows // seq
    head = width // HEADS
    nkeys = keys.shape[0]
    count = prompts.shape[0]
    scale = head ** (-0.5)
    parts = [pl.ds(part * width, width) for part in range(3)]
    for k in range(seq):
        tbuf[k] = toks[k][...]
    live = jnp.where(me < images, 1.0, 0.0)
    for c in range(seq):
        x[pl.ds(c * chunk, chunk), :] = tbuf[me ^ c].astype(F32) * live
    x_bf[...] = x[...].astype(BF16)
    mrow = mask[pl.ds(jnp.minimum(me, images - 1), 1), :].astype(F32)
    mcol = dot_tn(
        jnp.broadcast_to(mrow, (8, rows)).astype(BF16), jnp.full((8, rows), 0.125, BF16)
    )
    rest = lax.broadcasted_iota(jnp.int32, (nkeys - rows, rows), 0)
    bias[:rows, :] = jnp.where(mcol > 0.5, 0.0, -jnp.inf)
    bias[rows:, :] = jnp.where(rest < count, 0.0, -jnp.inf)
    hat, _ = normalize(x[...])
    normed[:rows, :] = (hat * gain_one[...] + shift_one[...]).astype(BF16)
    hat, _ = normalize(prompts[...].astype(BF16).astype(F32))
    normed[rows:, :] = jnp.zeros((nkeys - rows, width), BF16)
    normed[rows : rows + count, :] = (hat * gain_one[...] + shift_one[...]).astype(BF16)
    query[...] = (dot(normed[:rows, :], w_qkv[:, parts[0]]) + b_qkv[:, parts[0]]).astype(BF16)
    for index, dest in ((1, keys), (2, values)):
        part = parts[index]
        dest[...] = (dot(normed[...], w_qkv[:, part]) + b_qkv[:, part]).astype(BF16)
    lane = lax.broadcasted_iota(jnp.int32, (rows, 2 * head), 1) // head
    for h in range(HEADS):
        cols = pl.ds(h // 2 * 2 * head, 2 * head)
        qp = query[:, cols]
        qm = jnp.where(lane == h % 2, qp, jnp.zeros_like(qp))
        score = dot_nt(keys[:, cols], qm) * (scale * LOG2E) + bias[...]
        ex = jnp.exp2(score - jnp.max(score, axis=0, keepdims=True))
        prob = ex * (1.0 / jnp.sum(ex, axis=0, keepdims=True))
        p_f[h] = prob
        p_bf[h] = prob.astype(BF16)
    for h in range(HEADS):
        both = dot_tn(values[:, pl.ds(h // 2 * 2 * head, 2 * head)], p_bf[h])
        mix_t[pl.ds(h * head, head), :] = both[h % 2 * head :][:head].astype(BF16)
    resid[...] = x[...] + dot_tn(mix_t[...], w_out[...]) + b_out[...]
    hat, _ = normalize(resid[...])
    normed_two[...] = (hat * gain_two[...] + shift_two[...]).astype(BF16)


def backward_kernel(seq, images, *refs):
    cots, refs = refs[:seq], refs[seq:]
    (
        query, values, p_f, p_bf, resid, normed_two, w_qkv, w_out, gain_two, w_up, b_up, w_down,
        prompts, gain_one,
        pgrad, act, dres, ds_bf, dmix,
        gbuf, tbuf, dhid, gkv,
    ) = refs
    me = lax.axis_index("seq")
    rows, width = resid.shape
    chunk = rows // seq
    head = width // HEADS
    ff = act.shape[1]
    nkeys = values.shape[0]
    count = prompts.shape[0]
    scale = head ** (-0.5)
    for k in range(seq):
        tbuf[k] = cots[k][...]
    live = jnp.where(me < images, 1.0, 0.0)
    for c in range(seq):
        gbuf[pl.ds(c * chunk, chunk), :] = tbuf[me ^ c].astype(F32) * live
    grad_out = gbuf[...].astype(BF16)
    step = 256
    for c in range(ff // step):
        cols = pl.ds(c * step, step)
        hidden = dot(normed_two[...], w_up[:, cols]) + b_up[:, cols]
        grad = dot_nt(grad_out, w_down[cols, :])
        cdf = 0.5 * (1.0 + lax.erf(hidden * math.sqrt(0.5)))
        act[:, cols] = (hidden * cdf).astype(BF16)
        pdf = jnp.exp(-0.5 * hidden * hidden) * (1.0 / math.sqrt(2.0 * math.pi))
        dhid[:, cols] = (grad * (cdf + hidden * pdf)).astype(BF16)
    hat_two, rstd_two = normalize(resid[...])
    grad_resid = gbuf[...] + norm_back(
        hat_two, rstd_two, gain_two[...], dot_nt(dhid[...], w_up[...])
    )
    dres[...] = grad_resid
    dmix[...] = dot_nt(dres[...].astype(BF16), w_out[...]).astype(BF16)
    lane = lax.broadcasted_iota(jnp.int32, (rows, 2 * head), 1) // head
    for h in range(HEADS):
        cols = pl.ds(h // 2 * 2 * head, 2 * head)
        gp = dmix[:, cols]
        dprob = dot_nt(values[:, cols], jnp.where(lane == h % 2, gp, jnp.zeros_like(gp)))
        prob = p_f[h]
        both = prob * dprob
        inner = jnp.sum(both, axis=0, keepdims=True)
        ds_bf[h] = ((both - prob * inner) * scale).astype(BF16)
    low = lax.broadcasted_iota(jnp.int32, (nkeys - rows, 2 * head), 1) < head
    for pair in range(HEADS // 2):
        cols = pl.ds(pair * 2 * head, 2 * head)
        for at, source, other in ((0, ds_bf, query), (width, p_bf, dmix)):
            two = jnp.concatenate([source[2 * pair, rows:, :], source[2 * pair + 1, rows:, :]], 0)
            both = dot(two, other[:, cols])
            gkv[:, pl.ds(at + pair * 2 * head, 2 * head)] = jnp.where(
                low, both[: nkeys - rows], both[nkeys - rows :]
            )
    pad = pgrad.shape[0]
    grad_kv = gkv[:pad, :]
    first = grad_kv.astype(BF16)
    left = grad_kv - first.astype(F32)
    second = left.astype(BF16)
    third = (left - second.astype(F32)).astype(BF16)
    w_kv = w_qkv[:, pl.ds(width, 2 * width)]
    three = dot_nt(jnp.concatenate([first, second, third], 0), w_kv)
    grad_normed = three[:pad] + three[pad : 2 * pad] + three[2 * pad :]
    hat_p, rstd_p = normalize(prompts[...].astype(BF16).astype(F32))
    part = norm_back(hat_p, rstd_p, gain_one[...], grad_normed[:count, :]).astype(pgrad.dtype)
    pgrad[...] = jnp.zeros_like(pgrad)
    pgrad[:count, :] = part


def rest_kernel(
    seq, act, resid, dres, p_bf, ds_bf, query, dmix, keys, x_bf, w_down, w_qkv, b_down, gain,
    out, grad, dqkv, q_t, wide, k_t,
):
    rows, width = query.shape
    head = width // HEADS
    chunk = out.shape[1]
    k_t[...] = keys[...].T
    low = lax.broadcasted_iota(jnp.int32, (rows, 2 * head), 1) < head
    for pair in range(HEADS // 2):
        cols = pl.ds(pair * 2 * head, 2 * head)
        for at, source, other in ((width, ds_bf, query), (2 * width, p_bf, dmix)):
            two = jnp.concatenate([source[2 * pair, :rows, :], source[2 * pair + 1, :rows, :]], 0)
            both = dot(two, other[:, cols])
            dqkv[:, pl.ds(at + pair * 2 * head, 2 * head)] = jnp.where(
                low, both[:rows], both[rows:]
            ).astype(BF16)
    for h in range(HEADS):
        part = pl.ds(h * head, head)
        q_t[part, :] = dot(k_t[part, :], ds_bf[h]).astype(BF16)
    dqkv[:, :width] = q_t[...].T
    wide[...] = resid[...] + dot(act[...], w_down[...]) + b_down[...]
    for c in range(seq):
        out[c] = wide[pl.ds(c * chunk, chunk), :].astype(BF16)
    hat, rstd = normalize(x_bf[...].astype(F32))
    wide[...] = dres[...] + norm_back(hat, rstd, gain[...], dot_nt(dqkv[...], w_qkv[...]))
    for c in range(seq):
        grad[c] = wide[pl.ds(c * chunk, chunk), :].astype(BF16)


def pack_kernel(seq, out, grad, after, *packs):
    me = lax.axis_index("seq")
    for k in range(seq):
        packs[k][0] = out[me ^ k]
        packs[k][1] = grad[me ^ k]


def tree(values):
    while len(values) > 1:
        values = [
            values[i] + values[i + 1] if i + 1 < len(values) else values[i]
            for i in range(0, len(values), 2)
        ]
    return values[0]


def combine_kernel(*refs):
    error, parts, (combined, keep, give) = refs[0], refs[1:-4], refs[-3:]
    half = keep.shape[1]
    count = error.shape[0]
    core = lax.rem(lax.axis_index("dp"), 2)
    combined[...] = tree([part[...].astype(F32) for part in parts])
    combined[:count, :] += error[:, 0, :]
    low, high = combined[:, :half], combined[:, half:]
    keep[...] = jnp.where(core == 0, low, high)
    give[...] = jnp.where(core == 0, high, low)


def add_kernel(*refs):
    parts, out = refs[:-1], refs[-1]
    out[...] = tree([part[...].astype(F32) for part in parts]).astype(out.dtype)


def final_kernel(seq, images, total, *refs):
    back, refs = refs[:seq], refs[seq:]
    (
        mine, other, combined, start_t, prompts, momentum,
        layer_out, input_grad, basis_t, right_t, error, new_momentum, new_prompts, prompt_copy,
        whole,
    ) = refs
    me = lax.axis_index("seq")
    for k in range(seq):
        @pl.when((me ^ k) < images)
        def _():
            layer_out[me ^ k] = back[k][0]
            input_grad[me ^ k] = back[k][1]
    half = mine.shape[1]
    count, width = prompts.shape
    rank = start_t.shape[0]
    core = lax.rem(lax.axis_index("dp"), 2)
    whole[:, :half] = jnp.where(core == 0, mine[...], other[...]).astype(F32)
    whole[:, half:width] = jnp.where(core == 0, other[...], mine[...]).astype(F32)
    whole[:, width:] = combined[...]
    left = dot_nt(start_t[...], whole[:, :width], HIGH)
    row = lax.broadcasted_iota(jnp.int32, left.shape, 0)
    for j in range(rank):
        pivot = left[j : j + 1, :]
        along = jnp.sum(left * pivot, axis=1, keepdims=True)
        inverse = lax.rsqrt(along[j : j + 1, :] + 1e-12)
        pivot = pivot * inverse
        left = jnp.where(
            row > j, left - (along * inverse) * pivot, jnp.where(row == j, pivot, left)
        )
    right = jnp.dot(left, whole[...], precision=HIGH, preferred_element_type=F32)
    outer = dot_tn(left, right, HIGH)[:count, :]
    error[:, 0, :] = combined[:count, :] - outer[:, width:]
    moved = MOMENTUM_DECAY * momentum[...] + outer[:, :width] / total
    fresh = prompts[...] - RATE_SCALE * math.sqrt(total) * moved
    basis_t[...] = left[:, :count]
    right_t[...] = right[:, :width]
    new_momentum[...] = moved
    new_prompts[...] = fresh
    prompt_copy[...] = fresh.astype(BF16)


def flip(k, n):
    return [(i, i ^ k) for i in range(n)]


def body(
    tokens,
    key_mask,
    prompts,
    gain_one,
    shift_one,
    w_qkv,
    b_qkv,
    w_out,
    b_out,
    gain_two,
    shift_two,
    w_up,
    b_up,
    w_down,
    b_down,
    cotangent,
    start_factor,
    error_buffer,
    momentum,
):
    images, chunk, width = tokens.shape
    seq = lax.axis_size("seq")
    dp = lax.axis_size("dp")
    rows = seq * chunk
    ff = w_up.shape[1]
    count = prompts.shape[0]
    if images > seq or seq & (seq - 1) or dp & (dp - 1):
        raise ValueError("unsupported mesh")
    nkeys = up(rows + count, 16)
    pad = up(count, 8)
    dma = pltpu.SemaphoreType.DMA

    piece = ((2, chunk, width), BF16)
    one = ((chunk, width), BF16)
    row = lambda v: ((1, v.size), v.dtype) if v.ndim == 1 else (v.shape, v.dtype)
    small = (
        key_mask, prompts, gain_one, shift_one, b_qkv, b_out, gain_two, shift_two, b_up, b_down,
        error_buffer.transpose(1, 0, 2),
    )

    def pick(source, small, flops):
        return call(
            functools.partial(pick_kernel, seq, images, len(small)),
            [one] * seq + [row(v) for v in small],
            (source, *small),
            [dma((seq + len(small),))],
            in_specs=[HBM] * (1 + len(small)),
            flops=flops,
            name="pick",
        )

    toks = pick(tokens, (), 0)
    picked = pick(cotangent, small, 1 << 34)
    cots, small = picked[:seq], picked[seq:]
    mask, prompts_held, gain_one, shift_one, b_qkv, b_out, gain_two, shift_two = small[:8]
    b_up, b_down, error_rows = small[8:]
    toks = [toks[0]] + [lax.ppermute(toks[k], "seq", flip(k, seq)) for k in range(1, seq)]
    cots = [cots[0]] + [lax.ppermute(cots[k], "seq", flip(k, seq)) for k in range(1, seq)]

    wide = ((rows, width), BF16)
    long = ((nkeys, width), BF16)
    probs = (HEADS, nkeys, rows)
    x_bf, query, keys, values, p_f, p_bf, resid, normed_two = call(
        functools.partial(forward_kernel, seq, images),
        [wide, wide, long, long, (probs, F32), (probs, BF16), ((rows, width), F32), wide],
        (
            *toks, mask, prompts_held, gain_one, shift_one, b_qkv, b_out, gain_two, shift_two,
            w_qkv, w_out,
        ),
        [
            pltpu.VMEM((rows, width), F32),
            pltpu.VMEM((seq, chunk, width), BF16),
            pltpu.VMEM((nkeys, width), BF16),
            pltpu.VMEM((nkeys, rows), F32),
            pltpu.VMEM((width, rows), BF16),
        ],
        flops=2 * rows * width * (4 * width + 2 * nkeys),
        vmem=8 * MIB,
        name="forward",
    )

    wire = BF16
    pgrad, act, dres, ds_bf, dmix = call(
        functools.partial(backward_kernel, seq, images),
        [
            ((pad, width), wire), ((rows, ff), BF16), ((rows, width), F32), (probs, BF16), wide,
        ],
        (
            *cots, query, values, p_f, p_bf, resid, normed_two, w_qkv, w_out, gain_two,
            w_up, b_up, w_down, prompts_held, gain_one,
        ),
        [
            pltpu.VMEM((rows, width), F32),
            pltpu.VMEM((seq, chunk, width), BF16),
            pltpu.VMEM((rows, ff), BF16),
            pltpu.VMEM((nkeys - rows, 2 * width), F32),
        ],
        flops=2 * rows * width * (3 * width + 3 * ff),
        vmem=8 * MIB,
        name="backward",
    )
    kept = (act, resid, dres, p_bf, ds_bf, query, dmix, keys, x_bf)

    out_chunks, grad_chunks = call(
        functools.partial(rest_kernel, seq),
        [((seq, chunk, width), BF16)] * 2,
        (*kept, w_down, w_qkv, b_down, gain_one),
        [
            pltpu.VMEM((rows, 3 * width), BF16),
            pltpu.VMEM((width, rows), BF16),
            pltpu.VMEM((rows, width), F32),
            pltpu.VMEM((width, nkeys), BF16),
        ],
        flops=2 * rows * width * (3 * width + ff),
        vmem=8 * MIB,
        name="rest",
    )

    parts = [pgrad] + [lax.ppermute(pgrad, "seq", flip(k, seq)) for k in range(1, seq)]
    half = width // 2
    combined, keep, give = call(
        combine_kernel,
        [((pad, width), F32), ((pad, half), F32), ((pad, half), F32)],
        (error_rows, *parts, out_chunks),
        in_specs=[VMEM] * (1 + seq) + [ANY],
        name="combine",
    )
    parts = [keep, lax.ppermute(give, "dp", flip(1, dp))]
    bit = 2
    first = None
    while bit < dp:
        (mine,) = call(add_kernel, [((pad, half), wire)], parts, name="add")
        first = mine if first is None else first
        parts = [mine, lax.ppermute(mine, "dp", flip(bit, dp))]
        bit *= 2
    (mine,) = call(add_kernel, [((pad, half), F32)], parts, name="add")
    other = lax.ppermute(mine, "dp", flip(1, dp))

    packs = call(
        functools.partial(pack_kernel, seq),
        [piece] * seq,
        (out_chunks, grad_chunks, first),
        in_specs=[VMEM] * 2 + [ANY],
        flops=1 << 32,
        name="pack",
    )
    back = [packs[0]] + [
        lax.ppermute(packs[k], "seq", flip(k, seq)) for k in range(1, seq)
    ]
    rank = start_factor.shape[1]
    layer_out, input_grad, basis_t, right_t, error, new_momentum, new_prompts, prompt_copy = call(
        functools.partial(final_kernel, seq, images, images * dp),
        [
            ((images, chunk, width), BF16),
            ((images, chunk, width), BF16),
            ((rank, count), F32),
            ((rank, width), F32),
            ((count, 1, width), F32),
            ((count, width), F32),
            ((count, width), F32),
            ((count, width), BF16),
        ],
        (*back, mine, other, combined, start_factor.T, prompts, momentum),
        [pltpu.VMEM((pad, 2 * width), F32)],
        out_specs=[pl.BlockSpec(memory_space=pltpu.VMEM) for _ in range(8)],
        name="final",
    )
    return (
        layer_out,
        input_grad,
        basis_t.T,
        right_t.T,
        error.transpose(1, 0, 2),
        new_momentum,
        new_prompts,
        prompt_copy,
    )


def solution(mesh):
    rep = P()
    rows = P("dp", "seq", None)
    placed = (rows, P("dp", None), *([rep] * 13), rows, rep, P("dp", None, None), rep)
    return jax.shard_map(
        body,
        mesh=mesh,
        in_specs=placed,
        out_specs=(rows, rows, rep, rep, P("dp", None, None), rep, rep, rep),
        check_vma=False,
    )
```

```python
import functools
import math

import jax
import jax.numpy as jnp
from jax import lax
from jax.experimental import pallas as pl
from jax.experimental.pallas import tpu as pltpu
from jax.sharding import PartitionSpec as P

HEADS = 12
EPS = 1e-06
MOMENTUM_DECAY = 0.5
RATE_SCALE = 3.0
HIGH = lax.Precision.HIGH
F32 = jnp.float32
BF16 = jnp.bfloat16
VMEM = pl.BlockSpec(memory_space=pltpu.VMEM)
ANY = pl.BlockSpec(memory_space=pl.ANY)
HBM = pl.BlockSpec(memory_space=pltpu.HBM)
MIB = 1 << 20
LOG2E = 1.4426950408889634


def up(value, unit):
    return -(-value // unit) * unit


def dot(a, b):
    return jnp.dot(a, b, preferred_element_type=F32)


def dot_nt(a, b, precision=None):
    return lax.dot_general(
        a, b, (((1,), (1,)), ((), ())), precision=precision, preferred_element_type=F32
    )


def dot_tn(a, b, precision=None):
    return lax.dot_general(
        a, b, (((0,), (0,)), ((), ())), precision=precision, preferred_element_type=F32
    )


def normalize(values):
    center = values - jnp.mean(values, axis=-1, keepdims=True)
    rstd = lax.rsqrt(jnp.mean(center * center, axis=-1, keepdims=True) + EPS)
    return center * rstd, rstd


def norm_back(hat, rstd, gain, grad):
    inner = grad * gain
    mean = jnp.mean(inner, axis=-1, keepdims=True)
    along = jnp.mean(inner * hat, axis=-1, keepdims=True)
    return rstd * (inner - mean - hat * along)


def call(kernel, outs, ins, scratch=(), in_specs=None, out_specs=None, flops=0, vmem=8 * MIB, name=None):
    in_specs = in_specs or [VMEM] * len(ins)
    out_specs = out_specs or [VMEM] * len(outs)
    ins = [
        pltpu.with_memory_space_constraint(x, pltpu.HBM) if spec is HBM else x
        for x, spec in zip(ins, in_specs)
    ]
    held = {id(VMEM): pltpu.VMEM, id(HBM): pltpu.HBM}
    return pl.pallas_call(
        kernel,
        out_shape=[
            held.get(id(spec), jax.ShapeDtypeStruct)(s, d) for (s, d), spec in zip(outs, out_specs)
        ],
        in_specs=in_specs,
        out_specs=out_specs,
        scratch_shapes=list(scratch),
        compiler_params=pltpu.CompilerParams(vmem_limit_bytes=vmem),
        cost_estimate=pl.CostEstimate(
            flops=flops,
            bytes_accessed=sum(x.size * x.dtype.itemsize for x in ins),
            transcendentals=0,
        ),
        name=name,
    )(*ins)


class Copies:
    def __init__(self, sems):
        self.sems = sems
        self.used = 0

    def __call__(self, source, target):
        copy = pltpu.make_async_copy(source, target, self.sems.at[self.used])
        self.used += 1
        copy.start()
        return copy


def wait(*copies):
    for copy in copies:
        copy.wait()


def pick_kernel(seq, images, tok, cot, *refs):
    outs, sems = refs[:-1], refs[-1]
    me = lax.axis_index("seq")
    start = Copies(sems)
    copies = []
    for part, source in enumerate((tok, cot)):
        for k in range(seq):
            index = jnp.minimum(me ^ k, images - 1)
            copies.append(start(source.at[index], outs[part * seq + k]))
    wait(*copies)


def line(ref):
    return ref[...].reshape(1, -1)


def forward_kernel(seq, images, *refs):
    toks, refs = refs[:seq], refs[seq:]
    (
        mask, prompts, gain_one, shift_one, b_qkv, b_out, gain_two, shift_two, w_qkv, w_out, w_down,
        x_bf, query, keys, values, p_f, p_bf, resid, normed_two, w_down_t,
        x, tbuf, normed, bias, mix_t,
    ) = refs
    me = lax.axis_index("seq")
    gain, shift, bias_qkv = line(gain_one), line(shift_one), line(b_qkv)
    rows, width = x.shape
    chunk = rows // seq
    head = width // HEADS
    nkeys = keys.shape[0]
    count = prompts.shape[0]
    scale = head ** (-0.5)
    parts = [pl.ds(part * width, width) for part in range(3)]
    for k in range(seq):
        tbuf[(seq - k) % seq] = toks[k][...]
    live = jnp.where(me < images, 1.0, 0.0)
    for c in range(seq):
        x[pl.ds(c * chunk, chunk), :] = tbuf[me ^ c].astype(F32) * live
    x_bf[...] = x[...].astype(BF16)
    mrow = mask[pl.ds(jnp.minimum(me, images - 1), 1), :].astype(F32)
    mcol = dot_tn(
        jnp.broadcast_to(mrow, (8, rows)).astype(BF16), jnp.full((8, rows), 0.125, BF16)
    )
    rest = lax.broadcasted_iota(jnp.int32, (nkeys - rows, rows), 0)
    bias[:rows, :] = jnp.where(mcol > 0.5, 0.0, -jnp.inf)
    bias[rows:, :] = jnp.where(rest < count, 0.0, -jnp.inf)
    hat, _ = normalize(x[...])
    normed[:rows, :] = (hat * gain + shift).astype(BF16)
    hat, _ = normalize(prompts[...].astype(BF16).astype(F32))
    normed[rows:, :] = jnp.zeros((nkeys - rows, width), BF16)
    normed[rows : rows + count, :] = (hat * gain + shift).astype(BF16)
    query[...] = (dot(normed[:rows, :], w_qkv[:, parts[0]]) + bias_qkv[:, :width]).astype(BF16)
    for index, dest in ((1, keys), (2, values)):
        part = parts[index]
        dest[...] = (dot(normed[...], w_qkv[:, part]) + bias_qkv[:, index * width : (index + 1) * width]).astype(BF16)
    lane = lax.broadcasted_iota(jnp.int32, (rows, 2 * head), 1) // head
    for h in range(HEADS):
        cols = pl.ds(h // 2 * 2 * head, 2 * head)
        qp = query[:, cols]
        qm = jnp.where(lane == h % 2, qp, jnp.zeros_like(qp))
        score = dot_nt(keys[:, cols], qm) * (scale * LOG2E) + bias[...]
        ex = jnp.exp2(score - jnp.max(score, axis=0, keepdims=True))
        prob = ex * (1.0 / jnp.sum(ex, axis=0, keepdims=True))
        p_f[h] = prob
        p_bf[h] = prob.astype(BF16)
        slab = w_down.shape[0] // HEADS
        w_down_t[:, pl.ds(h * slab, slab)] = w_down[pl.ds(h * slab, slab), :].T
    for h in range(HEADS):
        both = dot_tn(values[:, pl.ds(h // 2 * 2 * head, 2 * head)], p_bf[h])
        mix_t[pl.ds(h * head, head), :] = both[h % 2 * head :][:head].astype(BF16)
    resid[...] = x[...] + dot_tn(mix_t[...], w_out[...]) + line(b_out)
    hat, _ = normalize(resid[...])
    normed_two[...] = (hat * line(gain_two) + line(shift_two)).astype(BF16)


def backward_kernel(seq, images, *refs):
    cots, refs = refs[:seq], refs[seq:]
    (
        query, values, p_f, p_bf, resid, normed_two, w_qkv, w_out, gain_two, w_up, b_up, w_down,
        prompts, gain_one,
        pgrad, act, dres, ds_bf, dmix,
        gbuf, tbuf, dhid, gkv,
    ) = refs
    me = lax.axis_index("seq")
    rows, width = resid.shape
    chunk = rows // seq
    head = width // HEADS
    ff = act.shape[1]
    nkeys = values.shape[0]
    count = prompts.shape[0]
    scale = head ** (-0.5)
    for k in range(seq):
        tbuf[(seq - k) % seq] = cots[k][...]
    live = jnp.where(me < images, 1.0, 0.0)
    for c in range(seq):
        gbuf[pl.ds(c * chunk, chunk), :] = tbuf[me ^ c].astype(F32) * live
    grad_out = gbuf[...].astype(BF16)
    bias_up = line(b_up)
    step = 256
    for c in range(ff // step):
        cols = pl.ds(c * step, step)
        hidden = dot(normed_two[...], w_up[:, cols]) + bias_up[:, c * step : (c + 1) * step]
        grad = dot(grad_out, w_down[:, cols])
        cdf = 0.5 * (1.0 + lax.erf(hidden * math.sqrt(0.5)))
        act[:, cols] = (hidden * cdf).astype(BF16)
        pdf = jnp.exp(-0.5 * hidden * hidden) * (1.0 / math.sqrt(2.0 * math.pi))
        dhid[:, cols] = (grad * (cdf + hidden * pdf)).astype(BF16)
    hat_two, rstd_two = normalize(resid[...])
    grad_resid = gbuf[...] + norm_back(
        hat_two, rstd_two, line(gain_two), dot_nt(dhid[...], w_up[...])
    )
    dres[...] = grad_resid
    dmix[...] = dot_nt(dres[...].astype(BF16), w_out[...]).astype(BF16)
    lane = lax.broadcasted_iota(jnp.int32, (rows, 2 * head), 1) // head
    for h in range(HEADS):
        cols = pl.ds(h // 2 * 2 * head, 2 * head)
        gp = dmix[:, cols]
        dprob = dot_nt(values[:, cols], jnp.where(lane == h % 2, gp, jnp.zeros_like(gp)))
        prob = p_f[h]
        both = prob * dprob
        inner = jnp.sum(both, axis=0, keepdims=True)
        ds_bf[h] = ((both - prob * inner) * scale).astype(BF16)
    low = lax.broadcasted_iota(jnp.int32, (nkeys - rows, 2 * head), 1) < head
    for pair in range(HEADS // 2):
        cols = pl.ds(pair * 2 * head, 2 * head)
        for at, source, other in ((0, ds_bf, query), (width, p_bf, dmix)):
            two = jnp.concatenate([source[2 * pair, rows:, :], source[2 * pair + 1, rows:, :]], 0)
            both = dot(two, other[:, cols])
            gkv[:, pl.ds(at + pair * 2 * head, 2 * head)] = jnp.where(
                low, both[: nkeys - rows], both[nkeys - rows :]
            )
    pad = pgrad.shape[0]
    grad_kv = gkv[:pad, :]
    first = grad_kv.astype(BF16)
    left = grad_kv - first.astype(F32)
    second = left.astype(BF16)
    third = (left - second.astype(F32)).astype(BF16)
    w_kv = w_qkv[:, pl.ds(width, 2 * width)]
    three = dot_nt(jnp.concatenate([first, second, third], 0), w_kv)
    grad_normed = three[:pad] + three[pad : 2 * pad] + three[2 * pad :]
    hat_p, rstd_p = normalize(prompts[...].astype(BF16).astype(F32))
    part = norm_back(hat_p, rstd_p, line(gain_one), grad_normed[:count, :]).astype(pgrad.dtype)
    pgrad[...] = jnp.zeros_like(pgrad)
    pgrad[:count, :] = part


def spans(chunk):
    full = chunk // 16 * 16
    return ((0, full), (full, chunk)) if full < chunk else ((0, full),)


def rest_kernel(
    seq, act, resid, dres, p_bf, ds_bf, query, dmix, keys, x_bf, w_down, w_qkv, b_down, gain,
    pack, dqkv, q_t, wide, k_t,
):
    rows, width = query.shape
    head = width // HEADS
    chunk = rows // seq
    full = spans(chunk)[0][1]
    k_t[...] = keys[...].T
    low = lax.broadcasted_iota(jnp.int32, (rows, 2 * head), 1) < head
    for pair in range(HEADS // 2):
        cols = pl.ds(pair * 2 * head, 2 * head)
        for at, source, other in ((width, ds_bf, query), (2 * width, p_bf, dmix)):
            two = jnp.concatenate([source[2 * pair, :rows, :], source[2 * pair + 1, :rows, :]], 0)
            both = dot(two, other[:, cols])
            dqkv[:, pl.ds(at + pair * 2 * head, 2 * head)] = jnp.where(
                low, both[:rows], both[rows:]
            ).astype(BF16)
    for h in range(HEADS):
        part = pl.ds(h * head, head)
        q_t[part, :] = dot(k_t[part, :], ds_bf[h]).astype(BF16)
    dqkv[:, :width] = q_t[...].T
    wide[...] = resid[...] + dot(act[...], w_down[...]) + line(b_down)
    for c in range(seq):
        for (low, high), at in zip(spans(chunk), (0, 2 * full)):
            pack[c, pl.ds(at, high - low), :] = wide[pl.ds(c * chunk + low, high - low), :].astype(
                BF16
            )
    hat, rstd = normalize(x_bf[...].astype(F32))
    wide[...] = dres[...] + norm_back(hat, rstd, line(gain), dot_nt(dqkv[...], w_qkv[...]))
    for c in range(seq):
        for (low, high), at in zip(spans(chunk), (full, full + chunk)):
            pack[c, pl.ds(at, high - low), :] = wide[pl.ds(c * chunk + low, high - low), :].astype(
                BF16
            )


def pack_kernel(seq, pack, after, *packs):
    me = lax.axis_index("seq")
    for k in range(seq):
        packs[k][...] = pack[me ^ k]


def tree(values):
    while len(values) > 1:
        values = [
            values[i] + values[i + 1] if i + 1 < len(values) else values[i]
            for i in range(0, len(values), 2)
        ]
    return values[0]


def combine_kernel(*refs):
    error, parts, (combined, keep, give) = refs[0], refs[1:-4], refs[-3:]
    half = keep.shape[1]
    count = error.shape[0]
    core = lax.rem(lax.axis_index("dp"), 2)
    combined[...] = tree([part[...].astype(F32) for part in parts])
    combined[:count, :] += error[:, 0, :]
    low, high = combined[:, :half], combined[:, half:]
    keep[...] = jnp.where(core == 0, low, high)
    give[...] = jnp.where(core == 0, high, low)


def add_kernel(*refs):
    parts, out = refs[:-1], refs[-1]
    out[...] = tree([part[...].astype(F32) for part in parts]).astype(out.dtype)


def final_kernel(seq, images, total, *refs):
    back, refs = refs[:seq], refs[seq:]
    (
        mine, other, combined, start_t, prompts, momentum,
        layer_out, input_grad, basis_t, right_t, error, new_momentum, new_prompts, prompt_copy,
        whole,
    ) = refs
    me = lax.axis_index("seq")
    chunk = layer_out.shape[1]
    full = spans(chunk)[0][1]
    for k in range(seq):
        @pl.when((me ^ k) < images)
        def _():
            for target, places in ((layer_out, (0, 2 * full)), (input_grad, (full, full + chunk))):
                for (low, high), at in zip(spans(chunk), places):
                    target[me ^ k, pl.ds(low, high - low), :] = back[k][pl.ds(at, high - low), :]
    half = mine.shape[1]
    count, width = prompts.shape
    rank = start_t.shape[0]
    core = lax.rem(lax.axis_index("dp"), 2)
    whole[:, :half] = jnp.where(core == 0, mine[...], other[...]).astype(F32)
    whole[:, half:width] = jnp.where(core == 0, other[...], mine[...]).astype(F32)
    whole[:, width:] = combined[...]
    left = dot_nt(start_t[...], whole[:, :width], HIGH)
    row = lax.broadcasted_iota(jnp.int32, left.shape, 0)
    for j in range(rank):
        pivot = left[j : j + 1, :]
        along = jnp.sum(left * pivot, axis=1, keepdims=True)
        inverse = lax.rsqrt(along[j : j + 1, :] + 1e-12)
        pivot = pivot * inverse
        left = jnp.where(
            row > j, left - (along * inverse) * pivot, jnp.where(row == j, pivot, left)
        )
    right = jnp.dot(left, whole[...], precision=HIGH, preferred_element_type=F32)
    outer = dot_tn(left, right, HIGH)[:count, :]
    error[:, 0, :] = combined[:count, :] - outer[:, width:]
    moved = MOMENTUM_DECAY * momentum[...] + outer[:, :width] / total
    fresh = prompts[...] - RATE_SCALE * math.sqrt(total) * moved
    basis_t[...] = left[:, :count]
    right_t[...] = right[:, :width]
    new_momentum[...] = moved
    new_prompts[...] = fresh
    prompt_copy[...] = fresh.astype(BF16)


def flip(k, n):
    return [(i, i ^ k) for i in range(n)]


def body(
    tokens,
    key_mask,
    prompts,
    gain_one,
    shift_one,
    w_qkv,
    b_qkv,
    w_out,
    b_out,
    gain_two,
    shift_two,
    w_up,
    b_up,
    w_down,
    b_down,
    cotangent,
    start_factor,
    error_buffer,
    momentum,
):
    images, chunk, width = tokens.shape
    seq = lax.axis_size("seq")
    dp = lax.axis_size("dp")
    rows = seq * chunk
    ff = w_up.shape[1]
    count = prompts.shape[0]
    if images > seq or seq & (seq - 1) or dp & (dp - 1):
        raise ValueError("unsupported mesh")
    nkeys = up(rows + count, 16)
    pad = up(count, 8)
    dma = pltpu.SemaphoreType.DMA

    piece = ((2 * chunk, width), BF16)
    one = ((chunk, width), BF16)
    picked = call(
        functools.partial(pick_kernel, seq, images),
        [one] * (2 * seq),
        (tokens, cotangent),
        [dma((2 * seq,))],
        in_specs=[HBM] * 2,
        flops=1 << 34,
        name="pick",
    )
    toks, cots = picked[:seq], picked[seq:]
    error_rows = error_buffer.transpose(1, 0, 2)
    toks = [toks[0]] + [lax.ppermute(toks[k], "seq", flip(k, seq)) for k in range(seq - 1, 0, -1)]
    cots = [cots[0]] + [lax.ppermute(cots[k], "seq", flip(k, seq)) for k in range(seq - 1, 0, -1)]

    wide = ((rows, width), BF16)
    long = ((nkeys, width), BF16)
    probs = (HEADS, nkeys, rows)
    x_bf, query, keys, values, p_f, p_bf, resid, normed_two, w_down_t = call(
        functools.partial(forward_kernel, seq, images),
        [wide, wide, long, long, (probs, F32), (probs, BF16), ((rows, width), F32), wide, ((width, ff), BF16)],
        (
            *toks, key_mask, prompts, gain_one, shift_one, b_qkv, b_out, gain_two, shift_two,
            w_qkv, w_out, w_down,
        ),
        [
            pltpu.VMEM((rows, width), F32),
            pltpu.VMEM((seq, chunk, width), BF16),
            pltpu.VMEM((nkeys, width), BF16),
            pltpu.VMEM((nkeys, rows), F32),
            pltpu.VMEM((width, rows), BF16),
        ],
        flops=2 * rows * width * (4 * width + 2 * nkeys),
        vmem=8 * MIB,
        name="forward",
    )

    wire = BF16
    pgrad, act, dres, ds_bf, dmix = call(
        functools.partial(backward_kernel, seq, images),
        [
            ((pad, width), wire), ((rows, ff), BF16), ((rows, width), F32), (probs, BF16), wide,
        ],
        (
            *cots, query, values, p_f, p_bf, resid, normed_two, w_qkv, w_out, gain_two,
            w_up, b_up, w_down_t, prompts, gain_one,
        ),
        [
            pltpu.VMEM((rows, width), F32),
            pltpu.VMEM((seq, chunk, width), BF16),
            pltpu.VMEM((rows, ff), BF16),
            pltpu.VMEM((nkeys - rows, 2 * width), F32),
        ],
        flops=2 * rows * width * (3 * width + 3 * ff),
        vmem=8 * MIB,
        name="backward",
    )
    kept = (act, resid, dres, p_bf, ds_bf, query, dmix, keys, x_bf)

    (chunks,) = call(
        functools.partial(rest_kernel, seq),
        [((seq, 2 * chunk, width), BF16)],
        (*kept, w_down, w_qkv, b_down, gain_one),
        [
            pltpu.VMEM((rows, 3 * width), BF16),
            pltpu.VMEM((width, rows), BF16),
            pltpu.VMEM((rows, width), F32),
            pltpu.VMEM((width, nkeys), BF16),
        ],
        flops=2 * rows * width * (3 * width + ff),
        vmem=8 * MIB,
        name="rest",
    )

    parts = [pgrad] + [lax.ppermute(pgrad, "seq", flip(k, seq)) for k in range(1, seq)]
    half = width // 2
    combined, keep, give = call(
        combine_kernel,
        [((pad, width), F32), ((pad, half), F32), ((pad, half), F32)],
        (error_rows, *parts, chunks),
        in_specs=[VMEM] * (1 + seq) + [ANY],
        name="combine",
    )
    parts = [keep, lax.ppermute(give, "dp", flip(1, dp))]
    bit = 2
    first = None
    while bit < dp:
        (mine,) = call(add_kernel, [((pad, half), wire)], parts, name="add")
        first = mine if first is None else first
        parts = [mine, lax.ppermute(mine, "dp", flip(bit, dp))]
        bit *= 2
    (mine,) = call(add_kernel, [((pad, half), F32)], parts, name="add")
    other = lax.ppermute(mine, "dp", flip(1, dp))

    packs = call(
        functools.partial(pack_kernel, seq),
        [piece] * seq,
        (chunks, first),
        in_specs=[VMEM, ANY],
        flops=1 << 32,
        name="pack",
    )
    back = [packs[0]] + [
        lax.ppermute(packs[k], "seq", flip(k, seq)) for k in range(1, seq)
    ]
    rank = start_factor.shape[1]
    layer_out, input_grad, basis_t, right_t, error, new_momentum, new_prompts, prompt_copy = call(
        functools.partial(final_kernel, seq, images, images * dp),
        [
            ((images, chunk, width), BF16),
            ((images, chunk, width), BF16),
            ((rank, count), F32),
            ((rank, width), F32),
            ((count, 1, width), F32),
            ((count, width), F32),
            ((count, width), F32),
            ((count, width), BF16),
        ],
        (*back, mine, other, combined, start_factor.T, prompts, momentum),
        [pltpu.VMEM((pad, 2 * width), F32)],
        out_specs=[pl.BlockSpec(memory_space=pltpu.VMEM) for _ in range(8)],
        name="final",
    )
    return (
        layer_out,
        input_grad,
        basis_t.T,
        right_t.T,
        error.transpose(1, 0, 2),
        new_momentum,
        new_prompts,
        prompt_copy,
    )


def solution(mesh):
    rep = P()
    rows = P("dp", "seq", None)
    placed = (rows, P("dp", None), *([rep] * 13), rows, rep, P("dp", None, None), rep)
    return jax.shard_map(
        body,
        mesh=mesh,
        in_specs=placed,
        out_specs=(rows, rows, rep, rep, P("dp", None, None), rep, rep, rep),
        check_vma=False,
    )
```

```python
import functools
import math

import jax
import jax.numpy as jnp
from jax import lax
from jax.experimental import pallas as pl
from jax.experimental.pallas import tpu as pltpu
from jax.sharding import PartitionSpec as P

HEADS = 12
EPS = 1e-06
MOMENTUM_DECAY = 0.5
RATE_SCALE = 3.0
HIGH = lax.Precision.HIGH
F32 = jnp.float32
BF16 = jnp.bfloat16
VMEM = pl.BlockSpec(memory_space=pltpu.VMEM)
ANY = pl.BlockSpec(memory_space=pl.ANY)
HBM = pl.BlockSpec(memory_space=pltpu.HBM)
MIB = 1 << 20
LOG2E = 1.4426950408889634


def up(value, unit):
    return -(-value // unit) * unit


def dot(a, b):
    return jnp.dot(a, b, preferred_element_type=F32)


def dot_nt(a, b, precision=None):
    return lax.dot_general(
        a, b, (((1,), (1,)), ((), ())), precision=precision, preferred_element_type=F32
    )


def dot_tn(a, b, precision=None):
    return lax.dot_general(
        a, b, (((0,), (0,)), ((), ())), precision=precision, preferred_element_type=F32
    )


def normalize(values):
    center = values - jnp.mean(values, axis=-1, keepdims=True)
    rstd = lax.rsqrt(jnp.mean(center * center, axis=-1, keepdims=True) + EPS)
    return center * rstd, rstd


def norm_back(hat, rstd, gain, grad):
    inner = grad * gain
    mean = jnp.mean(inner, axis=-1, keepdims=True)
    along = jnp.mean(inner * hat, axis=-1, keepdims=True)
    return rstd * (inner - mean - hat * along)


def call(kernel, outs, ins, scratch=(), in_specs=None, out_specs=None, flops=0, vmem=8 * MIB, name=None):
    in_specs = in_specs or [VMEM] * len(ins)
    out_specs = out_specs or [VMEM] * len(outs)
    ins = [
        pltpu.with_memory_space_constraint(x, pltpu.HBM) if spec is HBM else x
        for x, spec in zip(ins, in_specs)
    ]
    held = {id(VMEM): pltpu.VMEM, id(HBM): pltpu.HBM}
    return pl.pallas_call(
        kernel,
        out_shape=[
            held.get(id(spec), jax.ShapeDtypeStruct)(s, d) for (s, d), spec in zip(outs, out_specs)
        ],
        in_specs=in_specs,
        out_specs=out_specs,
        scratch_shapes=list(scratch),
        compiler_params=pltpu.CompilerParams(vmem_limit_bytes=vmem),
        cost_estimate=pl.CostEstimate(
            flops=flops,
            bytes_accessed=sum(x.size * x.dtype.itemsize for x in ins),
            transcendentals=0,
        ),
        name=name,
    )(*ins)


class Copies:
    def __init__(self, sems):
        self.sems = sems
        self.used = 0

    def __call__(self, source, target):
        copy = pltpu.make_async_copy(source, target, self.sems.at[self.used])
        self.used += 1
        copy.start()
        return copy


def wait(*copies):
    for copy in copies:
        copy.wait()


def pick_kernel(seq, images, tok, cot, *refs):
    outs, sems = refs[:-1], refs[-1]
    me = lax.axis_index("seq")
    start = Copies(sems)
    copies = []
    for part, source in enumerate((tok, cot)):
        for k in range(seq):
            index = jnp.minimum(me ^ k, images - 1)
            copies.append(start(source.at[index], outs[part * seq + k]))
    wait(*copies)


def line(ref):
    return ref[...].reshape(1, -1)


def forward_kernel(seq, images, *refs):
    toks, refs = refs[:seq], refs[seq:]
    (
        mask, prompts, gain_one, shift_one, b_qkv, b_out, gain_two, shift_two, w_qkv, w_out, w_down,
        x_bf, query, keys, values, p_f, p_bf, resid, normed_two, w_down_t,
        x, tbuf, normed, bias, mix_t,
    ) = refs
    me = lax.axis_index("seq")
    gain, shift, bias_qkv = line(gain_one), line(shift_one), line(b_qkv)
    rows, width = x.shape
    chunk = rows // seq
    head = width // HEADS
    nkeys = keys.shape[0]
    count = prompts.shape[0]
    scale = head ** (-0.5)
    parts = [pl.ds(part * width, width) for part in range(3)]
    for k in range(seq):
        tbuf[(seq - k) % seq] = toks[k][...]
    live = jnp.where(me < images, 1.0, 0.0)
    for c in range(seq):
        x[pl.ds(c * chunk, chunk), :] = tbuf[me ^ c].astype(F32) * live
    x_bf[...] = x[...].astype(BF16)
    mrow = mask[pl.ds(jnp.minimum(me, images - 1), 1), :].astype(F32)
    mcol = dot_tn(
        jnp.broadcast_to(mrow, (8, rows)).astype(BF16), jnp.full((8, rows), 0.125, BF16)
    )
    rest = lax.broadcasted_iota(jnp.int32, (nkeys - rows, rows), 0)
    bias[:rows, :] = jnp.where(mcol > 0.5, 0.0, -jnp.inf)
    bias[rows:, :] = jnp.where(rest < count, 0.0, -jnp.inf)
    hat, _ = normalize(x[...])
    normed[:rows, :] = (hat * gain + shift).astype(BF16)
    hat, _ = normalize(prompts[...].astype(BF16).astype(F32))
    normed[rows:, :] = jnp.zeros((nkeys - rows, width), BF16)
    normed[rows : rows + count, :] = (hat * gain + shift).astype(BF16)
    query[...] = (dot(normed[:rows, :], w_qkv[:, parts[0]]) + bias_qkv[:, :width]).astype(BF16)
    for index, dest in ((1, keys), (2, values)):
        part = parts[index]
        dest[...] = (dot(normed[...], w_qkv[:, part]) + bias_qkv[:, index * width : (index + 1) * width]).astype(BF16)
    lane = lax.broadcasted_iota(jnp.int32, (rows, 2 * head), 1) // head
    for h in range(HEADS):
        cols = pl.ds(h // 2 * 2 * head, 2 * head)
        qp = query[:, cols]
        qm = jnp.where(lane == h % 2, qp, jnp.zeros_like(qp))
        score = dot_nt(keys[:, cols], qm) * (scale * LOG2E) + bias[...]
        ex = jnp.exp2(score - jnp.max(score, axis=0, keepdims=True))
        prob = ex * (1.0 / jnp.sum(ex, axis=0, keepdims=True))
        p_f[h] = prob
        p_bf[h] = prob.astype(BF16)
        slab = w_down.shape[0] // HEADS
        w_down_t[:, pl.ds(h * slab, slab)] = w_down[pl.ds(h * slab, slab), :].T
    for h in range(HEADS):
        part = pl.ds(h * head, head)
        mix_t[part, :] = dot_tn(values[:, part], p_bf[h]).astype(BF16)
    resid[...] = x[...] + dot_tn(mix_t[...], w_out[...]) + line(b_out)
    hat, _ = normalize(resid[...])
    normed_two[...] = (hat * line(gain_two) + line(shift_two)).astype(BF16)


def backward_kernel(seq, images, *refs):
    cots, refs = refs[:seq], refs[seq:]
    (
        query, values, p_f, p_bf, resid, normed_two, w_qkv, w_out, gain_two, w_up, b_up, w_down,
        prompts, gain_one,
        pgrad, act, dres, ds_bf, dmix,
        gbuf, tbuf, dhid, gkv,
    ) = refs
    me = lax.axis_index("seq")
    rows, width = resid.shape
    chunk = rows // seq
    head = width // HEADS
    ff = act.shape[1]
    nkeys = values.shape[0]
    count = prompts.shape[0]
    scale = head ** (-0.5)
    for k in range(seq):
        tbuf[(seq - k) % seq] = cots[k][...]
    live = jnp.where(me < images, 1.0, 0.0)
    for c in range(seq):
        gbuf[pl.ds(c * chunk, chunk), :] = tbuf[me ^ c].astype(F32) * live
    grad_out = gbuf[...].astype(BF16)
    bias_up = line(b_up)
    step = 256
    for c in range(ff // step):
        cols = pl.ds(c * step, step)
        hidden = dot(normed_two[...], w_up[:, cols]) + bias_up[:, c * step : (c + 1) * step]
        grad = dot(grad_out, w_down[:, cols])
        cdf = 0.5 * (1.0 + lax.erf(hidden * math.sqrt(0.5)))
        act[:, cols] = (hidden * cdf).astype(BF16)
        pdf = jnp.exp(-0.5 * hidden * hidden) * (1.0 / math.sqrt(2.0 * math.pi))
        dhid[:, cols] = (grad * (cdf + hidden * pdf)).astype(BF16)
    hat_two, rstd_two = normalize(resid[...])
    grad_resid = gbuf[...] + norm_back(
        hat_two, rstd_two, line(gain_two), dot_nt(dhid[...], w_up[...])
    )
    dres[...] = grad_resid
    dmix[...] = dot_nt(dres[...].astype(BF16), w_out[...]).astype(BF16)
    lane = lax.broadcasted_iota(jnp.int32, (nkeys, 2 * head), 1) // head
    for h in range(HEADS):
        cols = pl.ds(h // 2 * 2 * head, 2 * head)
        if h % 2 == 0:
            vp = values[:, cols]
            none = jnp.zeros_like(vp)
            two = jnp.concatenate([jnp.where(lane == side, vp, none) for side in range(2)], 0)
            dprobs = dot_nt(two, dmix[:, cols])
        dprob = dprobs[h % 2 * nkeys :][:nkeys]
        prob = p_f[h]
        both = prob * dprob
        inner = jnp.sum(both, axis=0, keepdims=True)
        ds_bf[h] = ((both - prob * inner) * scale).astype(BF16)
    low = lax.broadcasted_iota(jnp.int32, (nkeys - rows, 2 * head), 1) < head
    for pair in range(HEADS // 2):
        cols = pl.ds(pair * 2 * head, 2 * head)
        for at, source, other in ((0, ds_bf, query), (width, p_bf, dmix)):
            two = jnp.concatenate([source[2 * pair, rows:, :], source[2 * pair + 1, rows:, :]], 0)
            both = dot(two, other[:, cols])
            gkv[:, pl.ds(at + pair * 2 * head, 2 * head)] = jnp.where(
                low, both[: nkeys - rows], both[nkeys - rows :]
            )
    pad = pgrad.shape[0]
    grad_kv = gkv[:pad, :]
    first = grad_kv.astype(BF16)
    left = grad_kv - first.astype(F32)
    second = left.astype(BF16)
    third = (left - second.astype(F32)).astype(BF16)
    w_kv = w_qkv[:, pl.ds(width, 2 * width)]
    three = dot_nt(jnp.concatenate([first, second, third], 0), w_kv)
    grad_normed = three[:pad] + three[pad : 2 * pad] + three[2 * pad :]
    hat_p, rstd_p = normalize(prompts[...].astype(BF16).astype(F32))
    part = norm_back(hat_p, rstd_p, line(gain_one), grad_normed[:count, :]).astype(pgrad.dtype)
    pgrad[...] = jnp.zeros_like(pgrad)
    pgrad[:count, :] = part


def spans(chunk):
    full = chunk // 16 * 16
    return ((0, full), (full, chunk)) if full < chunk else ((0, full),)


def rest_kernel(
    seq, act, resid, dres, p_bf, ds_bf, query, dmix, keys, x_bf, w_down, w_qkv, b_down, gain,
    pack, dqkv, q_t, wide, k_t,
):
    rows, width = query.shape
    head = width // HEADS
    chunk = rows // seq
    full = spans(chunk)[0][1]
    k_t[...] = keys[...].T
    low = lax.broadcasted_iota(jnp.int32, (rows, 2 * head), 1) < head
    for pair in range(HEADS // 2):
        cols = pl.ds(pair * 2 * head, 2 * head)
        for at, source, other in ((width, ds_bf, query), (2 * width, p_bf, dmix)):
            two = jnp.concatenate([source[2 * pair, :rows, :], source[2 * pair + 1, :rows, :]], 0)
            both = dot(two, other[:, cols])
            dqkv[:, pl.ds(at + pair * 2 * head, 2 * head)] = jnp.where(
                low, both[:rows], both[rows:]
            ).astype(BF16)
    for h in range(HEADS):
        part = pl.ds(h * head, head)
        q_t[part, :] = dot(k_t[part, :], ds_bf[h]).astype(BF16)
    dqkv[:, :width] = q_t[...].T
    wide[...] = resid[...] + dot(act[...], w_down[...]) + line(b_down)
    for c in range(seq):
        for (low, high), at in zip(spans(chunk), (0, 2 * full)):
            pack[c, pl.ds(at, high - low), :] = wide[pl.ds(c * chunk + low, high - low), :].astype(
                BF16
            )
    hat, rstd = normalize(x_bf[...].astype(F32))
    wide[...] = dres[...] + norm_back(hat, rstd, line(gain), dot_nt(dqkv[...], w_qkv[...]))
    for c in range(seq):
        for (low, high), at in zip(spans(chunk), (full, full + chunk)):
            pack[c, pl.ds(at, high - low), :] = wide[pl.ds(c * chunk + low, high - low), :].astype(
                BF16
            )


def pack_kernel(ways, pack, after, *packs):
    me = lax.axis_index("seq")
    for k, out in zip(ways, packs):
        out[...] = pack[me ^ k]


def tree(values):
    while len(values) > 1:
        values = [
            values[i] + values[i + 1] if i + 1 < len(values) else values[i]
            for i in range(0, len(values), 2)
        ]
    return values[0]


def combine_kernel(*refs):
    error, parts, (combined, keep, give) = refs[0], refs[1:-4], refs[-3:]
    half = keep.shape[1]
    count = error.shape[0]
    core = lax.rem(lax.axis_index("dp"), 2)
    combined[...] = tree([part[...].astype(F32) for part in parts])
    combined[:count, :] += error[:, 0, :]
    low, high = combined[:, :half], combined[:, half:]
    keep[...] = jnp.where(core == 0, low, high)
    give[...] = jnp.where(core == 0, high, low)


def add_kernel(*refs):
    parts, out = refs[:-1], refs[-1]
    out[...] = tree([part[...].astype(F32) for part in parts]).astype(out.dtype)


def place_kernel(seq, images, *refs):
    back, (after, layer_out, input_grad) = refs[:seq], refs[seq:]
    me = lax.axis_index("seq")
    chunk = layer_out.shape[1]
    full = spans(chunk)[0][1]
    for k in range(seq):
        @pl.when((me ^ k) < images)
        def _():
            for target, places in ((layer_out, (0, 2 * full)), (input_grad, (full, full + chunk))):
                for (low, high), at in zip(spans(chunk), places):
                    target[me ^ k, pl.ds(low, high - low), :] = back[k][pl.ds(at, high - low), :]


def final_kernel(total, *refs):
    (
        mine, other, combined, start_t, prompts, momentum,
        basis_t, right_t, error, new_momentum, new_prompts, prompt_copy, done, whole,
    ) = refs[:6] + refs[-8:]
    half = mine.shape[1]
    count, width = prompts.shape
    rank = start_t.shape[0]
    core = lax.rem(lax.axis_index("dp"), 2)
    whole[:, :half] = jnp.where(core == 0, mine[...], other[...]).astype(F32)
    whole[:, half:width] = jnp.where(core == 0, other[...], mine[...]).astype(F32)
    whole[:, width:] = combined[...]
    left = dot_nt(start_t[...], whole[:, :width], HIGH)
    row = lax.broadcasted_iota(jnp.int32, left.shape, 0)
    for j in range(rank):
        pivot = left[j : j + 1, :]
        along = jnp.sum(left * pivot, axis=1, keepdims=True)
        inverse = lax.rsqrt(along[j : j + 1, :] + 1e-12)
        pivot = pivot * inverse
        left = jnp.where(
            row > j, left - (along * inverse) * pivot, jnp.where(row == j, pivot, left)
        )
    right = jnp.dot(left, whole[...], precision=HIGH, preferred_element_type=F32)
    outer = dot_tn(left, right, HIGH)[:count, :]
    error[:, 0, :] = combined[:count, :] - outer[:, width:]
    moved = MOMENTUM_DECAY * momentum[...] + outer[:, :width] / total
    fresh = prompts[...] - RATE_SCALE * math.sqrt(total) * moved
    basis_t[...] = left[:, :count]
    right_t[...] = right[:, :width]
    new_momentum[...] = moved
    new_prompts[...] = fresh
    prompt_copy[...] = fresh.astype(BF16)
    done[...] = jnp.zeros_like(done)


def flip(k, n):
    return [(i, i ^ k) for i in range(n)]


def body(
    tokens,
    key_mask,
    prompts,
    gain_one,
    shift_one,
    w_qkv,
    b_qkv,
    w_out,
    b_out,
    gain_two,
    shift_two,
    w_up,
    b_up,
    w_down,
    b_down,
    cotangent,
    start_factor,
    error_buffer,
    momentum,
):
    images, chunk, width = tokens.shape
    seq = lax.axis_size("seq")
    dp = lax.axis_size("dp")
    rows = seq * chunk
    ff = w_up.shape[1]
    count = prompts.shape[0]
    if images > seq or seq & (seq - 1) or dp & (dp - 1):
        raise ValueError("unsupported mesh")
    nkeys = up(rows + count, 16)
    pad = up(count, 8)
    dma = pltpu.SemaphoreType.DMA

    piece = ((2 * chunk, width), BF16)
    one = ((chunk, width), BF16)
    picked = call(
        functools.partial(pick_kernel, seq, images),
        [one] * (2 * seq),
        (tokens, cotangent),
        [dma((2 * seq,))],
        in_specs=[HBM] * 2,
        flops=1 << 34,
        name="pick",
    )
    toks, cots = picked[:seq], picked[seq:]
    error_rows = error_buffer.transpose(1, 0, 2)
    toks = [toks[0]] + [lax.ppermute(toks[k], "seq", flip(k, seq)) for k in range(seq - 1, 0, -1)]
    cots = [cots[0]] + [lax.ppermute(cots[k], "seq", flip(k, seq)) for k in range(seq - 1, 0, -1)]

    wide = ((rows, width), BF16)
    long = ((nkeys, width), BF16)
    probs = (HEADS, nkeys, rows)
    x_bf, query, keys, values, p_f, p_bf, resid, normed_two, w_down_t = call(
        functools.partial(forward_kernel, seq, images),
        [wide, wide, long, long, (probs, F32), (probs, BF16), ((rows, width), F32), wide, ((width, ff), BF16)],
        (
            *toks, key_mask, prompts, gain_one, shift_one, b_qkv, b_out, gain_two, shift_two,
            w_qkv, w_out, w_down,
        ),
        [
            pltpu.VMEM((rows, width), F32),
            pltpu.VMEM((seq, chunk, width), BF16),
            pltpu.VMEM((nkeys, width), BF16),
            pltpu.VMEM((nkeys, rows), F32),
            pltpu.VMEM((width, rows), BF16),
        ],
        flops=2 * rows * width * (4 * width + 2 * nkeys),
        vmem=8 * MIB,
        name="forward",
    )

    wire = BF16
    pgrad, act, dres, ds_bf, dmix = call(
        functools.partial(backward_kernel, seq, images),
        [
            ((pad, width), wire), ((rows, ff), BF16), ((rows, width), F32), (probs, BF16), wide,
        ],
        (
            *cots, query, values, p_f, p_bf, resid, normed_two, w_qkv, w_out, gain_two,
            w_up, b_up, w_down_t, prompts, gain_one,
        ),
        [
            pltpu.VMEM((rows, width), F32),
            pltpu.VMEM((seq, chunk, width), BF16),
            pltpu.VMEM((rows, ff), BF16),
            pltpu.VMEM((nkeys - rows, 2 * width), F32),
        ],
        flops=2 * rows * width * (3 * width + 3 * ff),
        vmem=8 * MIB,
        name="backward",
    )
    kept = (act, resid, dres, p_bf, ds_bf, query, dmix, keys, x_bf)

    (chunks,) = call(
        functools.partial(rest_kernel, seq),
        [((seq, 2 * chunk, width), BF16)],
        (*kept, w_down, w_qkv, b_down, gain_one),
        [
            pltpu.VMEM((rows, 3 * width), BF16),
            pltpu.VMEM((width, rows), BF16),
            pltpu.VMEM((rows, width), F32),
            pltpu.VMEM((width, nkeys), BF16),
        ],
        flops=2 * rows * width * (3 * width + ff),
        vmem=8 * MIB,
        name="rest",
    )

    parts = [pgrad] + [lax.ppermute(pgrad, "seq", flip(k, seq)) for k in range(1, seq)]
    half = width // 2
    combined, keep, give = call(
        combine_kernel,
        [((pad, width), F32), ((pad, half), F32), ((pad, half), F32)],
        (error_rows, *parts, chunks),
        in_specs=[VMEM] * (1 + seq) + [ANY],
        name="combine",
    )
    parts = [keep, lax.ppermute(give, "dp", flip(1, dp))]
    bit = 2
    sums = []
    while bit < dp:
        (mine,) = call(add_kernel, [((pad, half), wire)], parts, name="add")
        sums.append(mine)
        parts = [mine, lax.ppermute(mine, "dp", flip(bit, dp))]
        bit *= 2
    (mine,) = call(add_kernel, [((pad, half), F32)], parts, name="add")
    other = lax.ppermute(mine, "dp", flip(1, dp))

    groups = ((0,1,2), (3,)) if seq == 4 and len(sums) > 1 else (tuple(range(seq)), ())
    back = [None] * seq
    for ways, after in zip(groups, sums):
        packs = call(
            functools.partial(pack_kernel, ways),
            [piece] * len(ways),
            (chunks, after),
            in_specs=[VMEM, ANY],
            name="pack",
        )
        for k, pack in zip(ways, packs):
            back[k] = lax.ppermute(pack, "seq", flip(k, seq)) if k else pack

    rank = start_factor.shape[1]
    free = pl.BlockSpec(memory_space=pltpu.VMEM)
    early = [back[k] for k in groups[0] if k]
    basis_t, right_t, error, new_momentum, new_prompts, prompt_copy, done = call(
        functools.partial(final_kernel, images * dp),
        [
            ((rank, count), F32),
            ((rank, width), F32),
            ((count, 1, width), F32),
            ((count, width), F32),
            ((count, width), F32),
            ((count, width), BF16),
            ((8, 128), F32),
        ],
        (mine, other, combined, start_factor.T, prompts, momentum, *early),
        [pltpu.VMEM((pad, 2 * width), F32)],
        in_specs=[VMEM] * 6 + [ANY] * len(early),
        out_specs=[free] * 6 + [VMEM],
        flops=7 << 26,
        name="final",
    )
    layer_out, input_grad = call(
        functools.partial(place_kernel, seq, images),
        [((images, chunk, width), BF16)] * 2,
        (*back, done),
        in_specs=[VMEM] * seq + [ANY],
        out_specs=[free] * 2,
        name="place",
    )
    return (
        layer_out,
        input_grad,
        basis_t.T,
        right_t.T,
        error.transpose(1, 0, 2),
        new_momentum,
        new_prompts,
        prompt_copy,
    )


def solution(mesh):
    rep = P()
    rows = P("dp", "seq", None)
    placed = (rows, P("dp", None), *([rep] * 13), rows, rep, P("dp", None, None), rep)
    return jax.shard_map(
        body,
        mesh=mesh,
        in_specs=placed,
        out_specs=(rows, rows, rep, rep, P("dp", None, None), rep, rep, rep),
        check_vma=False,
    )
```

```python
import functools
import math

import jax
import jax.numpy as jnp
from jax import lax
from jax.experimental import pallas as pl
from jax.experimental.pallas import tpu as pltpu
from jax.sharding import PartitionSpec as P

HEADS = 12
EPS = 1e-06
MOMENTUM_DECAY = 0.5
RATE_SCALE = 3.0
HIGH = lax.Precision.HIGH
F32 = jnp.float32
BF16 = jnp.bfloat16
VMEM = pl.BlockSpec(memory_space=pltpu.VMEM)
ANY = pl.BlockSpec(memory_space=pl.ANY)
HBM = pl.BlockSpec(memory_space=pltpu.HBM)
MIB = 1 << 20
LOG2E = 1.4426950408889634


def up(value, unit):
    return -(-value // unit) * unit


def dot(a, b):
    return jnp.dot(a, b, preferred_element_type=F32)


def dot_nt(a, b, precision=None):
    return lax.dot_general(
        a, b, (((1,), (1,)), ((), ())), precision=precision, preferred_element_type=F32
    )


def dot_tn(a, b, precision=None):
    return lax.dot_general(
        a, b, (((0,), (0,)), ((), ())), precision=precision, preferred_element_type=F32
    )


def normalize(values):
    center = values - jnp.mean(values, axis=-1, keepdims=True)
    rstd = lax.rsqrt(jnp.mean(center * center, axis=-1, keepdims=True) + EPS)
    return center * rstd, rstd


def norm_back(hat, rstd, gain, grad):
    inner = grad * gain
    mean = jnp.mean(inner, axis=-1, keepdims=True)
    along = jnp.mean(inner * hat, axis=-1, keepdims=True)
    return rstd * (inner - mean - hat * along)


def call(kernel, outs, ins, scratch=(), in_specs=None, out_specs=None, flops=0, vmem=8 * MIB, name=None):
    in_specs = in_specs or [VMEM] * len(ins)
    out_specs = out_specs or [VMEM] * len(outs)
    ins = [
        pltpu.with_memory_space_constraint(x, pltpu.HBM) if spec is HBM else x
        for x, spec in zip(ins, in_specs)
    ]
    held = {id(VMEM): pltpu.VMEM, id(HBM): pltpu.HBM}
    return pl.pallas_call(
        kernel,
        out_shape=[
            held.get(id(spec), jax.ShapeDtypeStruct)(s, d) for (s, d), spec in zip(outs, out_specs)
        ],
        in_specs=in_specs,
        out_specs=out_specs,
        scratch_shapes=list(scratch),
        compiler_params=pltpu.CompilerParams(vmem_limit_bytes=vmem),
        cost_estimate=pl.CostEstimate(
            flops=flops,
            bytes_accessed=sum(x.size * x.dtype.itemsize for x in ins),
            transcendentals=0,
        ),
        name=name,
    )(*ins)


class Copies:
    def __init__(self, sems):
        self.sems = sems
        self.used = 0

    def __call__(self, source, target):
        copy = pltpu.make_async_copy(source, target, self.sems.at[self.used])
        self.used += 1
        copy.start()
        return copy


def wait(*copies):
    for copy in copies:
        copy.wait()


def pick_kernel(seq, images, tok, cot, *refs):
    outs, sems = refs[:-1], refs[-1]
    me = lax.axis_index("seq")
    start = Copies(sems)
    copies = []
    for part, source in enumerate((tok, cot)):
        for k in range(seq):
            index = jnp.minimum(me ^ k, images - 1)
            copies.append(start(source.at[index], outs[part * seq + k]))
    wait(*copies)


def line(ref):
    return ref[...].reshape(1, -1)


def forward_kernel(seq, images, *refs):
    toks, refs = refs[:seq], refs[seq:]
    (
        mask, prompts, gain_one, shift_one, b_qkv, b_out, gain_two, shift_two, w_qkv, w_out, w_down,
        x_bf, query, keys, values, p_f, p_bf, resid, normed_two, w_down_t,
        x, tbuf, normed, bias, mix_t,
    ) = refs
    me = lax.axis_index("seq")
    gain, shift, bias_qkv = line(gain_one), line(shift_one), line(b_qkv)
    rows, width = x.shape
    chunk = rows // seq
    head = width // HEADS
    nkeys = keys.shape[0]
    count = prompts.shape[0]
    scale = head ** (-0.5)
    parts = [pl.ds(part * width, width) for part in range(3)]
    for k in range(seq):
        tbuf[(seq - k) % seq] = toks[k][...]
    live = jnp.where(me < images, 1.0, 0.0)
    for c in range(seq):
        x[pl.ds(c * chunk, chunk), :] = tbuf[me ^ c].astype(F32) * live
    x_bf[...] = x[...].astype(BF16)
    mrow = mask[pl.ds(jnp.minimum(me, images - 1), 1), :].astype(F32)
    mcol = dot_tn(
        jnp.broadcast_to(mrow, (8, rows)).astype(BF16), jnp.full((8, rows), 0.125, BF16)
    )
    rest = lax.broadcasted_iota(jnp.int32, (nkeys - rows, rows), 0)
    bias[:rows, :] = jnp.where(mcol > 0.5, 0.0, -jnp.inf)
    bias[rows:, :] = jnp.where(rest < count, 0.0, -jnp.inf)
    hat, _ = normalize(x[...])
    normed[:rows, :] = (hat * gain + shift).astype(BF16)
    hat, _ = normalize(prompts[...].astype(BF16).astype(F32))
    normed[rows:, :] = jnp.zeros((nkeys - rows, width), BF16)
    normed[rows : rows + count, :] = (hat * gain + shift).astype(BF16)
    query[...] = (dot(normed[:rows, :], w_qkv[:, parts[0]]) + bias_qkv[:, :width]).astype(BF16)
    for index, dest in ((1, keys), (2, values)):
        part = parts[index]
        dest[...] = (dot(normed[...], w_qkv[:, part]) + bias_qkv[:, index * width : (index + 1) * width]).astype(BF16)
    lane = lax.broadcasted_iota(jnp.int32, (rows, 2 * head), 1) // head
    for h in range(HEADS):
        cols = pl.ds(h // 2 * 2 * head, 2 * head)
        qp = query[:, cols]
        qm = jnp.where(lane == h % 2, qp, jnp.zeros_like(qp))
        score = dot_nt(keys[:, cols], qm) * (scale * LOG2E) + bias[...]
        ex = jnp.exp2(score - jnp.max(score, axis=0, keepdims=True))
        prob = ex * (1.0 / jnp.sum(ex, axis=0, keepdims=True))
        p_f[h] = prob
        p_bf[h] = prob.astype(BF16)
        slab = w_down.shape[0] // HEADS
        w_down_t[:, pl.ds(h * slab, slab)] = w_down[pl.ds(h * slab, slab), :].T
    for h in range(HEADS):
        part = pl.ds(h * head, head)
        mix_t[part, :] = dot_tn(values[:, part], p_bf[h]).astype(BF16)
    resid[...] = x[...] + dot_tn(mix_t[...], w_out[...]) + line(b_out)
    hat, _ = normalize(resid[...])
    normed_two[...] = (hat * line(gain_two) + line(shift_two)).astype(BF16)


def backward_kernel(seq, images, *refs):
    cots, refs = refs[:seq], refs[seq:]
    (
        query, values, p_f, p_bf, resid, normed_two, w_qkv, w_out, gain_two, w_up, b_up, w_down,
        prompts, gain_one,
        pgrad, act, dres, ds_bf, dmix,
        gbuf, tbuf, dhid, gkv,
    ) = refs
    me = lax.axis_index("seq")
    rows, width = resid.shape
    chunk = rows // seq
    head = width // HEADS
    ff = act.shape[1]
    nkeys = values.shape[0]
    count = prompts.shape[0]
    scale = head ** (-0.5)
    for k in range(seq):
        tbuf[(seq - k) % seq] = cots[k][...]
    live = jnp.where(me < images, 1.0, 0.0)
    for c in range(seq):
        gbuf[pl.ds(c * chunk, chunk), :] = tbuf[me ^ c].astype(F32) * live
    grad_out = gbuf[...].astype(BF16)
    bias_up = line(b_up)
    step = 256
    for c in range(ff // step):
        cols = pl.ds(c * step, step)
        hidden = dot(normed_two[...], w_up[:, cols]) + bias_up[:, c * step : (c + 1) * step]
        grad = dot(grad_out, w_down[:, cols])
        cdf = 0.5 * (1.0 + lax.erf(hidden * math.sqrt(0.5)))
        act[:, cols] = (hidden * cdf).astype(BF16)
        pdf = jnp.exp(-0.5 * hidden * hidden) * (1.0 / math.sqrt(2.0 * math.pi))
        dhid[:, cols] = (grad * (cdf + hidden * pdf)).astype(BF16)
    hat_two, rstd_two = normalize(resid[...])
    grad_resid = gbuf[...] + norm_back(
        hat_two, rstd_two, line(gain_two), dot_nt(dhid[...], w_up[...])
    )
    dres[...] = grad_resid
    dmix[...] = dot_nt(dres[...].astype(BF16), w_out[...]).astype(BF16)
    lane = lax.broadcasted_iota(jnp.int32, (nkeys, 2 * head), 1) // head
    for h in range(HEADS):
        cols = pl.ds(h // 2 * 2 * head, 2 * head)
        if h % 2 == 0:
            vp = values[:, cols]
            none = jnp.zeros_like(vp)
            two = jnp.concatenate([jnp.where(lane == side, vp, none) for side in range(2)], 0)
            dprobs = dot_nt(two, dmix[:, cols])
        dprob = dprobs[h % 2 * nkeys :][:nkeys]
        prob = p_f[h]
        both = prob * dprob
        inner = jnp.sum(both, axis=0, keepdims=True)
        ds_bf[h] = ((both - prob * inner) * scale).astype(BF16)
    low = lax.broadcasted_iota(jnp.int32, (nkeys - rows, 2 * head), 1) < head
    for pair in range(HEADS // 2):
        cols = pl.ds(pair * 2 * head, 2 * head)
        for at, source, other in ((0, ds_bf, query), (width, p_bf, dmix)):
            two = jnp.concatenate([source[2 * pair, rows:, :], source[2 * pair + 1, rows:, :]], 0)
            both = dot(two, other[:, cols])
            gkv[:, pl.ds(at + pair * 2 * head, 2 * head)] = jnp.where(
                low, both[: nkeys - rows], both[nkeys - rows :]
            )
    pad = pgrad.shape[0]
    grad_kv = gkv[:pad, :]
    first = grad_kv.astype(BF16)
    left = grad_kv - first.astype(F32)
    second = left.astype(BF16)
    third = (left - second.astype(F32)).astype(BF16)
    w_kv = w_qkv[:, pl.ds(width, 2 * width)]
    three = dot_nt(jnp.concatenate([first, second, third], 0), w_kv)
    grad_normed = three[:pad] + three[pad : 2 * pad] + three[2 * pad :]
    hat_p, rstd_p = normalize(prompts[...].astype(BF16).astype(F32))
    part = norm_back(hat_p, rstd_p, line(gain_one), grad_normed[:count, :]).astype(pgrad.dtype)
    pgrad[...] = jnp.zeros_like(pgrad)
    pgrad[:count, :] = part


def spans(chunk):
    full = chunk // 16 * 16
    return ((0, full), (full, chunk)) if full < chunk else ((0, full),)


def rest_kernel(
    seq, act, resid, dres, p_bf, ds_bf, query, dmix, keys, x_bf, w_down, w_qkv, b_down, gain,
    pack, dqkv, q_t, wide,
):
    rows, width = query.shape
    head = width // HEADS
    chunk = rows // seq
    full = spans(chunk)[0][1]
    low = lax.broadcasted_iota(jnp.int32, (rows, 2 * head), 1) < head
    for pair in range(HEADS // 2):
        cols = pl.ds(pair * 2 * head, 2 * head)
        for at, source, other in ((width, ds_bf, query), (2 * width, p_bf, dmix)):
            two = jnp.concatenate([source[2 * pair, :rows, :], source[2 * pair + 1, :rows, :]], 0)
            both = dot(two, other[:, cols])
            dqkv[:, pl.ds(at + pair * 2 * head, 2 * head)] = jnp.where(
                low, both[:rows], both[rows:]
            ).astype(BF16)
    for h in range(HEADS):
        part = pl.ds(h * head, head)
        q_t[part, :] = dot_tn(keys[:, part], ds_bf[h]).astype(BF16)
    dqkv[:, :width] = q_t[...].T
    wide[...] = resid[...] + dot(act[...], w_down[...]) + line(b_down)
    for c in range(seq):
        for (low, high), at in zip(spans(chunk), (0, 2 * full)):
            pack[c, pl.ds(at, high - low), :] = wide[pl.ds(c * chunk + low, high - low), :].astype(
                BF16
            )
    hat, rstd = normalize(x_bf[...].astype(F32))
    wide[...] = dres[...] + norm_back(hat, rstd, line(gain), dot_nt(dqkv[...], w_qkv[...]))
    for c in range(seq):
        for (low, high), at in zip(spans(chunk), (full, full + chunk)):
            pack[c, pl.ds(at, high - low), :] = wide[pl.ds(c * chunk + low, high - low), :].astype(
                BF16
            )


def pack_kernel(seq, pack, after, *packs):
    me = lax.axis_index("seq")
    for k in range(seq):
        packs[k][...] = pack[me ^ k]


def tree(values):
    while len(values) > 1:
        values = [
            values[i] + values[i + 1] if i + 1 < len(values) else values[i]
            for i in range(0, len(values), 2)
        ]
    return values[0]


def combine_kernel(*refs):
    error, parts, (combined, keep, give) = refs[0], refs[1:-4], refs[-3:]
    half = keep.shape[1]
    count = error.shape[0]
    core = lax.rem(lax.axis_index("dp"), 2)
    combined[...] = tree([part[...].astype(F32) for part in parts])
    combined[:count, :] += error[:, 0, :]
    low, high = combined[:, :half], combined[:, half:]
    keep[...] = jnp.where(core == 0, low, high).astype(keep.dtype)
    give[...] = jnp.where(core == 0, high, low).astype(give.dtype)


def add_kernel(*refs):
    parts, out = refs[:-1], refs[-1]
    out[...] = tree([part[...].astype(F32) for part in parts]).astype(out.dtype)


def final_kernel(seq, images, total, *refs):
    back, refs = refs[:seq], refs[seq:]
    (
        mine, other, combined, start_t, prompts, momentum,
        layer_out, input_grad, basis_t, right_t, error, new_momentum, new_prompts, prompt_copy,
        whole,
    ) = refs
    me = lax.axis_index("seq")
    chunk = layer_out.shape[1]
    full = spans(chunk)[0][1]
    for k in range(seq):
        @pl.when((me ^ k) < images)
        def _():
            for target, places in ((layer_out, (0, 2 * full)), (input_grad, (full, full + chunk))):
                for (low, high), at in zip(spans(chunk), places):
                    target[me ^ k, pl.ds(low, high - low), :] = back[(seq - k) % seq][
                        pl.ds(at, high - low), :
                    ]
    half = mine.shape[1]
    count, width = prompts.shape
    rank = start_t.shape[0]
    core = lax.rem(lax.axis_index("dp"), 2)
    whole[:, :half] = jnp.where(core == 0, mine[...], other[...]).astype(F32)
    whole[:, half:width] = jnp.where(core == 0, other[...], mine[...]).astype(F32)
    whole[:, width:] = combined[...]
    left = dot_nt(start_t[...], whole[:, :width], HIGH)
    row = lax.broadcasted_iota(jnp.int32, left.shape, 0)
    for j in range(rank):
        pivot = left[j : j + 1, :]
        along = jnp.sum(left * pivot, axis=1, keepdims=True)
        inverse = lax.rsqrt(along[j : j + 1, :] + 1e-12)
        pivot = pivot * inverse
        left = jnp.where(
            row > j, left - (along * inverse) * pivot, jnp.where(row == j, pivot, left)
        )
    right = jnp.dot(left, whole[...], precision=HIGH, preferred_element_type=F32)
    outer = dot_tn(left, right, HIGH)[:count, :]
    error[:, 0, :] = combined[:count, :] - outer[:, width:]
    moved = MOMENTUM_DECAY * momentum[...] + outer[:, :width] / total
    fresh = prompts[...] - RATE_SCALE * math.sqrt(total) * moved
    basis_t[...] = left[:, :count]
    right_t[...] = right[:, :width]
    new_momentum[...] = moved
    new_prompts[...] = fresh
    prompt_copy[...] = fresh.astype(BF16)


def flip(k, n):
    return [(i, i ^ k) for i in range(n)]


def body(
    tokens,
    key_mask,
    prompts,
    gain_one,
    shift_one,
    w_qkv,
    b_qkv,
    w_out,
    b_out,
    gain_two,
    shift_two,
    w_up,
    b_up,
    w_down,
    b_down,
    cotangent,
    start_factor,
    error_buffer,
    momentum,
):
    images, chunk, width = tokens.shape
    seq = lax.axis_size("seq")
    dp = lax.axis_size("dp")
    rows = seq * chunk
    ff = w_up.shape[1]
    count = prompts.shape[0]
    if images > seq or seq & (seq - 1) or dp & (dp - 1):
        raise ValueError("unsupported mesh")
    nkeys = up(rows + count, 16)
    pad = up(count, 8)
    dma = pltpu.SemaphoreType.DMA

    piece = ((2 * chunk, width), BF16)
    one = ((chunk, width), BF16)
    picked = call(
        functools.partial(pick_kernel, seq, images),
        [one] * (2 * seq),
        (tokens, cotangent),
        [dma((2 * seq,))],
        in_specs=[HBM] * 2,
        flops=1 << 34,
        name="pick",
    )
    toks, cots = picked[:seq], picked[seq:]
    error_rows = error_buffer.transpose(1, 0, 2)
    toks = [toks[0]] + [lax.ppermute(toks[k], "seq", flip(k, seq)) for k in range(seq - 1, 0, -1)]
    cots = [cots[0]] + [lax.ppermute(cots[k], "seq", flip(k, seq)) for k in range(seq - 1, 0, -1)]

    wide = ((rows, width), BF16)
    long = ((nkeys, width), BF16)
    probs = (HEADS, nkeys, rows)
    x_bf, query, keys, values, p_f, p_bf, resid, normed_two, w_down_t = call(
        functools.partial(forward_kernel, seq, images),
        [wide, wide, long, long, (probs, F32), (probs, BF16), ((rows, width), F32), wide, ((width, ff), BF16)],
        (
            *toks, key_mask, prompts, gain_one, shift_one, b_qkv, b_out, gain_two, shift_two,
            w_qkv, w_out, w_down,
        ),
        [
            pltpu.VMEM((rows, width), F32),
            pltpu.VMEM((seq, chunk, width), BF16),
            pltpu.VMEM((nkeys, width), BF16),
            pltpu.VMEM((nkeys, rows), F32),
            pltpu.VMEM((width, rows), BF16),
        ],
        flops=2 * rows * width * (4 * width + 2 * nkeys),
        vmem=8 * MIB,
        name="forward",
    )

    wire = BF16
    pgrad, act, dres, ds_bf, dmix = call(
        functools.partial(backward_kernel, seq, images),
        [
            ((pad, width), wire), ((rows, ff), BF16), ((rows, width), F32), (probs, BF16), wide,
        ],
        (
            *cots, query, values, p_f, p_bf, resid, normed_two, w_qkv, w_out, gain_two,
            w_up, b_up, w_down_t, prompts, gain_one,
        ),
        [
            pltpu.VMEM((rows, width), F32),
            pltpu.VMEM((seq, chunk, width), BF16),
            pltpu.VMEM((rows, ff), BF16),
            pltpu.VMEM((nkeys - rows, 2 * width), F32),
        ],
        flops=2 * rows * width * (3 * width + 3 * ff),
        vmem=8 * MIB,
        name="backward",
    )
    kept = (act, resid, dres, p_bf, ds_bf, query, dmix, keys, x_bf)

    (chunks,) = call(
        functools.partial(rest_kernel, seq),
        [((seq, 2 * chunk, width), BF16)],
        (*kept, w_down, w_qkv, b_down, gain_one),
        [
            pltpu.VMEM((rows, 3 * width), BF16),
            pltpu.VMEM((width, rows), BF16),
            pltpu.VMEM((rows, width), F32),
        ],
        flops=2 * rows * width * (3 * width + ff),
        vmem=8 * MIB,
        name="rest",
    )

    parts = [pgrad] + [lax.ppermute(pgrad, "seq", flip(k, seq)) for k in range(1, seq)]
    half = width // 2
    combined, keep, give = call(
        combine_kernel,
        [((pad, width), F32), ((pad, half), wire), ((pad, half), wire)],
        (error_rows, *parts, chunks),
        in_specs=[VMEM] * (1 + seq) + [ANY],
        name="combine",
    )
    parts = [keep, lax.ppermute(give, "dp", flip(1, dp))]
    if dp > 2:
        parts += [lax.ppermute(keep, "dp", flip(2, dp)), lax.ppermute(give, "dp", flip(3, dp))]
    bit = 4
    while bit < dp:
        (mine,) = call(add_kernel, [((pad, half), wire)], parts, name="add")
        parts = [mine, lax.ppermute(mine, "dp", flip(bit, dp))]
        bit *= 2
    (mine,) = call(add_kernel, [((pad, half), F32)], parts, name="add")
    other = lax.ppermute(mine, "dp", flip(1, dp))

    packs = call(
        functools.partial(pack_kernel, seq),
        [piece] * seq,
        (chunks, keep),
        in_specs=[VMEM, ANY],
        name="pack",
    )
    back = [packs[0]] + [lax.ppermute(packs[k], "seq", flip(k, seq)) for k in range(seq - 1, 0, -1)]

    rank = start_factor.shape[1]
    layer_out, input_grad, basis_t, right_t, error, new_momentum, new_prompts, prompt_copy = call(
        functools.partial(final_kernel, seq, images, images * dp),
        [
            ((images, chunk, width), BF16),
            ((images, chunk, width), BF16),
            ((rank, count), F32),
            ((rank, width), F32),
            ((count, 1, width), F32),
            ((count, width), F32),
            ((count, width), F32),
            ((count, width), BF16),
        ],
        (*back, mine, other, combined, start_factor.T, prompts, momentum),
        [pltpu.VMEM((pad, 2 * width), F32)],
        out_specs=[pl.BlockSpec(memory_space=pltpu.VMEM) for _ in range(8)],
        name="final",
    )
    return (
        layer_out,
        input_grad,
        basis_t.T,
        right_t.T,
        error.transpose(1, 0, 2),
        new_momentum,
        new_prompts,
        prompt_copy,
    )


def solution(mesh):
    rep = P()
    rows = P("dp", "seq", None)
    placed = (rows, P("dp", None), *([rep] * 13), rows, rep, P("dp", None, None), rep)
    return jax.shard_map(
        body,
        mesh=mesh,
        in_specs=placed,
        out_specs=(rows, rows, rep, rep, P("dp", None, None), rep, rep, rep),
        check_vma=False,
    )
```

```python
import functools
import math

import jax
import jax.numpy as jnp
from jax import lax
from jax.experimental import pallas as pl
from jax.experimental.pallas import tpu as pltpu
from jax.sharding import PartitionSpec as P

HEADS = 12
EPS = 1e-06
MOMENTUM_DECAY = 0.5
RATE_SCALE = 3.0
HIGH = lax.Precision.HIGH
F32 = jnp.float32
BF16 = jnp.bfloat16
VMEM = pl.BlockSpec(memory_space=pltpu.VMEM)
ANY = pl.BlockSpec(memory_space=pl.ANY)
HBM = pl.BlockSpec(memory_space=pltpu.HBM)
MIB = 1 << 20
LOG2E = 1.4426950408889634


def up(value, unit):
    return -(-value // unit) * unit


def dot(a, b):
    return jnp.dot(a, b, preferred_element_type=F32)


def dot_nt(a, b, precision=None):
    return lax.dot_general(
        a, b, (((1,), (1,)), ((), ())), precision=precision, preferred_element_type=F32
    )


def dot_tn(a, b, precision=None):
    return lax.dot_general(
        a, b, (((0,), (0,)), ((), ())), precision=precision, preferred_element_type=F32
    )


def normalize(values):
    center = values - jnp.mean(values, axis=-1, keepdims=True)
    rstd = lax.rsqrt(jnp.mean(center * center, axis=-1, keepdims=True) + EPS)
    return center * rstd, rstd


def norm_back(hat, rstd, gain, grad):
    inner = grad * gain
    mean = jnp.mean(inner, axis=-1, keepdims=True)
    along = jnp.mean(inner * hat, axis=-1, keepdims=True)
    return rstd * (inner - mean - hat * along)


def bands(rows):
    band = 16 if rows % 16 == 0 else 8 if rows % 8 == 0 else rows
    return [pl.ds(low, band) for low in range(0, rows, band)]


def call(kernel, outs, ins, scratch=(), in_specs=None, out_specs=None, flops=0, vmem=8 * MIB, name=None):
    in_specs = in_specs or [VMEM] * len(ins)
    out_specs = out_specs or [VMEM] * len(outs)
    ins = [
        pltpu.with_memory_space_constraint(x, pltpu.HBM) if spec is HBM else x
        for x, spec in zip(ins, in_specs)
    ]
    held = {id(VMEM): pltpu.VMEM, id(HBM): pltpu.HBM}
    return pl.pallas_call(
        kernel,
        out_shape=[
            held.get(id(spec), jax.ShapeDtypeStruct)(s, d) for (s, d), spec in zip(outs, out_specs)
        ],
        in_specs=in_specs,
        out_specs=out_specs,
        scratch_shapes=list(scratch),
        compiler_params=pltpu.CompilerParams(vmem_limit_bytes=vmem),
        cost_estimate=pl.CostEstimate(
            flops=flops,
            bytes_accessed=sum(x.size * x.dtype.itemsize for x in ins),
            transcendentals=0,
        ),
        name=name,
    )(*ins)


class Copies:
    def __init__(self, sems):
        self.sems = sems
        self.used = 0

    def __call__(self, source, target):
        copy = pltpu.make_async_copy(source, target, self.sems.at[self.used])
        self.used += 1
        copy.start()
        return copy


def wait(*copies):
    for copy in copies:
        copy.wait()


def pick_kernel(seq, images, tok, cot, *refs):
    outs, sems = refs[:-1], refs[-1]
    me = lax.axis_index("seq")
    start = Copies(sems)
    copies = []
    for part, source in enumerate((tok, cot)):
        for k in range(seq):
            index = jnp.minimum(me ^ k, images - 1)
            copies.append(start(source.at[index], outs[part * seq + k]))
    wait(*copies)


def line(ref):
    return ref[...].reshape(1, -1)


def forward_kernel(seq, images, *refs):
    toks, refs = refs[:seq], refs[seq:]
    (
        mask, prompts, gain_one, shift_one, b_qkv, b_out, gain_two, shift_two, w_qkv, w_out, w_down,
        x_bf, query, keys, values, p_f, p_bf, resid, normed_two, w_down_t,
        x, tbuf, normed, bias, mix_t,
    ) = refs
    me = lax.axis_index("seq")
    gain, shift, bias_qkv = line(gain_one), line(shift_one), line(b_qkv)
    rows, width = x.shape
    chunk = rows // seq
    head = width // HEADS
    nkeys = keys.shape[0]
    count = prompts.shape[0]
    scale = head ** (-0.5)
    parts = [pl.ds(part * width, width) for part in range(3)]
    for k in range(seq):
        tbuf[(seq - k) % seq] = toks[k][...]
    live = jnp.where(me < images, 1.0, 0.0)
    for c in range(seq):
        x[pl.ds(c * chunk, chunk), :] = tbuf[me ^ c].astype(F32) * live
    mrow = mask[pl.ds(jnp.minimum(me, images - 1), 1), :].astype(F32)
    mcol = dot_tn(
        jnp.broadcast_to(mrow, (8, rows)).astype(BF16), jnp.full((8, rows), 0.125, BF16)
    )
    rest = lax.broadcasted_iota(jnp.int32, (nkeys - rows, rows), 0)
    bias[:rows, :] = jnp.where(mcol > 0.5, 0.0, -jnp.inf)
    bias[rows:, :] = jnp.where(rest < count, 0.0, -jnp.inf)
    for band in bands(rows):
        x_bf[band, :] = x[band, :].astype(BF16)
        hat, _ = normalize(x[band, :])
        normed[band, :] = (hat * gain + shift).astype(BF16)
    hat, _ = normalize(prompts[...].astype(BF16).astype(F32))
    normed[rows:, :] = jnp.zeros((nkeys - rows, width), BF16)
    normed[rows : rows + count, :] = (hat * gain + shift).astype(BF16)
    query[...] = (dot(normed[:rows, :], w_qkv[:, parts[0]]) + bias_qkv[:, :width]).astype(BF16)
    for index, dest in ((1, keys), (2, values)):
        part = parts[index]
        dest[...] = (dot(normed[...], w_qkv[:, part]) + bias_qkv[:, index * width : (index + 1) * width]).astype(BF16)
    lane = lax.broadcasted_iota(jnp.int32, (rows, 2 * head), 1) // head
    for h in range(HEADS):
        cols = pl.ds(h // 2 * 2 * head, 2 * head)
        qp = query[:, cols]
        qm = jnp.where(lane == h % 2, qp, jnp.zeros_like(qp))
        score = dot_nt(keys[:, cols], qm) * (scale * LOG2E) + bias[...]
        ex = jnp.exp2(score - jnp.max(score, axis=0, keepdims=True))
        prob = ex * (1.0 / jnp.sum(ex, axis=0, keepdims=True))
        p_f[h] = prob
        p_bf[h] = prob.astype(BF16)
        slab = w_down.shape[0] // HEADS
        w_down_t[:, pl.ds(h * slab, slab)] = w_down[pl.ds(h * slab, slab), :].T
    for h in range(HEADS):
        part = pl.ds(h * head, head)
        mix_t[part, :] = dot_tn(values[:, part], p_bf[h]).astype(BF16)
    resid[...] = x[...] + dot_tn(mix_t[...], w_out[...]) + line(b_out)
    scale_two, offset_two = line(gain_two), line(shift_two)
    for band in bands(rows):
        hat, _ = normalize(resid[band, :])
        normed_two[band, :] = (hat * scale_two + offset_two).astype(BF16)


def backward_kernel(seq, images, *refs):
    cots, refs = refs[:seq], refs[seq:]
    (
        query, values, p_f, p_bf, resid, normed_two, w_qkv, w_out, gain_two, w_up, b_up, w_down,
        prompts, gain_one,
        pgrad, act, dres, ds_bf, dmix,
        gbuf, tbuf, dhid, gkv,
    ) = refs
    me = lax.axis_index("seq")
    rows, width = resid.shape
    chunk = rows // seq
    head = width // HEADS
    ff = act.shape[1]
    nkeys = values.shape[0]
    count = prompts.shape[0]
    scale = head ** (-0.5)
    for k in range(seq):
        tbuf[(seq - k) % seq] = cots[k][...]
    live = jnp.where(me < images, 1.0, 0.0)
    for c in range(seq):
        gbuf[pl.ds(c * chunk, chunk), :] = tbuf[me ^ c].astype(F32) * live
    grad_out = gbuf[...].astype(BF16)
    bias_up = line(b_up)
    step = 256
    for c in range(ff // step):
        cols = pl.ds(c * step, step)
        hidden = dot(normed_two[...], w_up[:, cols]) + bias_up[:, c * step : (c + 1) * step]
        grad = dot(grad_out, w_down[:, cols])
        cdf = 0.5 * (1.0 + lax.erf(hidden * math.sqrt(0.5)))
        act[:, cols] = (hidden * cdf).astype(BF16)
        pdf = jnp.exp(-0.5 * hidden * hidden) * (1.0 / math.sqrt(2.0 * math.pi))
        dhid[:, cols] = (grad * (cdf + hidden * pdf)).astype(BF16)
    dres[...] = dot_nt(dhid[...], w_up[...])
    scale_two = line(gain_two)
    for band in bands(rows):
        hat, rstd = normalize(resid[band, :])
        dres[band, :] = gbuf[band, :] + norm_back(hat, rstd, scale_two, dres[band, :])
    dmix[...] = dot_nt(dres[...].astype(BF16), w_out[...]).astype(BF16)
    lane = lax.broadcasted_iota(jnp.int32, (nkeys, 2 * head), 1) // head
    for h in range(HEADS):
        cols = pl.ds(h // 2 * 2 * head, 2 * head)
        if h % 2 == 0:
            vp = values[:, cols]
            none = jnp.zeros_like(vp)
            two = jnp.concatenate([jnp.where(lane == side, vp, none) for side in range(2)], 0)
            dprobs = dot_nt(two, dmix[:, cols])
        dprob = dprobs[h % 2 * nkeys :][:nkeys]
        prob = p_f[h]
        both = prob * dprob
        inner = jnp.sum(both, axis=0, keepdims=True)
        ds_bf[h] = ((both - prob * inner) * scale).astype(BF16)
    low = lax.broadcasted_iota(jnp.int32, (nkeys - rows, 2 * head), 1) < head
    for pair in range(HEADS // 2):
        cols = pl.ds(pair * 2 * head, 2 * head)
        for at, source, other in ((0, ds_bf, query), (width, p_bf, dmix)):
            two = jnp.concatenate([source[2 * pair, rows:, :], source[2 * pair + 1, rows:, :]], 0)
            both = dot(two, other[:, cols])
            gkv[:, pl.ds(at + pair * 2 * head, 2 * head)] = jnp.where(
                low, both[: nkeys - rows], both[nkeys - rows :]
            )
    pad = pgrad.shape[0]
    grad_kv = gkv[:pad, :]
    first = grad_kv.astype(BF16)
    left = grad_kv - first.astype(F32)
    second = left.astype(BF16)
    third = (left - second.astype(F32)).astype(BF16)
    w_kv = w_qkv[:, pl.ds(width, 2 * width)]
    three = dot_nt(jnp.concatenate([first, second, third], 0), w_kv)
    grad_normed = three[:pad] + three[pad : 2 * pad] + three[2 * pad :]
    hat_p, rstd_p = normalize(prompts[...].astype(BF16).astype(F32))
    part = norm_back(hat_p, rstd_p, line(gain_one), grad_normed[:count, :]).astype(pgrad.dtype)
    pgrad[...] = jnp.zeros_like(pgrad)
    pgrad[:count, :] = part


def spans(chunk):
    full = chunk // 16 * 16
    return ((0, full), (full, chunk)) if full < chunk else ((0, full),)


def rest_kernel(
    seq, act, resid, dres, p_bf, ds_bf, query, dmix, keys, x_bf, w_down, w_qkv, b_down, gain,
    pack, dqkv, q_t, wide,
):
    rows, width = query.shape
    head = width // HEADS
    chunk = rows // seq
    full = spans(chunk)[0][1]
    low = lax.broadcasted_iota(jnp.int32, (rows, 2 * head), 1) < head
    for pair in range(HEADS // 2):
        cols = pl.ds(pair * 2 * head, 2 * head)
        for at, source, other in ((width, ds_bf, query), (2 * width, p_bf, dmix)):
            two = jnp.concatenate([source[2 * pair, :rows, :], source[2 * pair + 1, :rows, :]], 0)
            both = dot(two, other[:, cols])
            dqkv[:, pl.ds(at + pair * 2 * head, 2 * head)] = jnp.where(
                low, both[:rows], both[rows:]
            ).astype(BF16)
    for h in range(HEADS):
        part = pl.ds(h * head, head)
        q_t[part, :] = dot_tn(keys[:, part], ds_bf[h]).astype(BF16)
    dqkv[:, :width] = q_t[...].T
    wide[...] = resid[...] + dot(act[...], w_down[...]) + line(b_down)
    for c in range(seq):
        for (low, high), at in zip(spans(chunk), (0, 2 * full)):
            pack[c, pl.ds(at, high - low), :] = wide[pl.ds(c * chunk + low, high - low), :].astype(
                BF16
            )
    wide[...] = dot_nt(dqkv[...], w_qkv[...])
    scale_one = line(gain)
    for band in bands(rows):
        hat, rstd = normalize(x_bf[band, :].astype(F32))
        wide[band, :] = dres[band, :] + norm_back(hat, rstd, scale_one, wide[band, :])
    for c in range(seq):
        for (low, high), at in zip(spans(chunk), (full, full + chunk)):
            pack[c, pl.ds(at, high - low), :] = wide[pl.ds(c * chunk + low, high - low), :].astype(
                BF16
            )


def pack_kernel(seq, pack, after, *packs):
    me = lax.axis_index("seq")
    for k in range(seq):
        packs[k][...] = pack[me ^ k]


def tree(values):
    while len(values) > 1:
        values = [
            values[i] + values[i + 1] if i + 1 < len(values) else values[i]
            for i in range(0, len(values), 2)
        ]
    return values[0]


def combine_kernel(*refs):
    error, parts, (combined, keep, give) = refs[0], refs[1:-4], refs[-3:]
    half = keep.shape[1]
    count = error.shape[0]
    core = lax.rem(lax.axis_index("dp"), 2)
    combined[...] = tree([part[...].astype(F32) for part in parts])
    combined[:count, :] += error[:, 0, :]
    low, high = combined[:, :half], combined[:, half:]
    keep[...] = jnp.where(core == 0, low, high).astype(keep.dtype)
    give[...] = jnp.where(core == 0, high, low).astype(give.dtype)


def add_kernel(*refs):
    parts, out = refs[:-1], refs[-1]
    out[...] = tree([part[...].astype(F32) for part in parts]).astype(out.dtype)


def final_kernel(seq, images, total, *refs):
    back, refs = refs[:seq], refs[seq:]
    (
        mine, other, combined, start_t, prompts, momentum,
        layer_out, input_grad, basis_t, right_t, error, new_momentum, new_prompts, prompt_copy,
        whole,
    ) = refs
    me = lax.axis_index("seq")
    chunk = layer_out.shape[1]
    full = spans(chunk)[0][1]
    for k in range(seq):
        @pl.when((me ^ k) < images)
        def _():
            for target, places in ((layer_out, (0, 2 * full)), (input_grad, (full, full + chunk))):
                for (low, high), at in zip(spans(chunk), places):
                    target[me ^ k, pl.ds(low, high - low), :] = back[(seq - k) % seq][
                        pl.ds(at, high - low), :
                    ]
    half = mine.shape[1]
    count, width = prompts.shape
    rank = start_t.shape[0]
    core = lax.rem(lax.axis_index("dp"), 2)
    whole[:, :half] = jnp.where(core == 0, mine[...], other[...]).astype(F32)
    whole[:, half:width] = jnp.where(core == 0, other[...], mine[...]).astype(F32)
    whole[:, width:] = combined[...]
    left = dot_nt(start_t[...], whole[:, :width], HIGH)
    row = lax.broadcasted_iota(jnp.int32, left.shape, 0)
    for j in range(rank):
        pivot = left[j : j + 1, :]
        along = jnp.sum(left * pivot, axis=1, keepdims=True)
        inverse = lax.rsqrt(along[j : j + 1, :] + 1e-12)
        pivot = pivot * inverse
        left = jnp.where(
            row > j, left - (along * inverse) * pivot, jnp.where(row == j, pivot, left)
        )
    right = jnp.dot(left, whole[...], precision=HIGH, preferred_element_type=F32)
    outer = dot_tn(left, right, HIGH)[:count, :]
    error[:, 0, :] = combined[:count, :] - outer[:, width:]
    moved = MOMENTUM_DECAY * momentum[...] + outer[:, :width] / total
    fresh = prompts[...] - RATE_SCALE * math.sqrt(total) * moved
    basis_t[...] = left[:, :count]
    right_t[...] = right[:, :width]
    new_momentum[...] = moved
    new_prompts[...] = fresh
    prompt_copy[...] = fresh.astype(BF16)


def flip(k, n):
    return [(i, i ^ k) for i in range(n)]


def body(
    tokens,
    key_mask,
    prompts,
    gain_one,
    shift_one,
    w_qkv,
    b_qkv,
    w_out,
    b_out,
    gain_two,
    shift_two,
    w_up,
    b_up,
    w_down,
    b_down,
    cotangent,
    start_factor,
    error_buffer,
    momentum,
):
    images, chunk, width = tokens.shape
    seq = lax.axis_size("seq")
    dp = lax.axis_size("dp")
    rows = seq * chunk
    ff = w_up.shape[1]
    count = prompts.shape[0]
    if images > seq or seq & (seq - 1) or dp & (dp - 1):
        raise ValueError("unsupported mesh")
    nkeys = up(rows + count, 16)
    pad = up(count, 8)
    dma = pltpu.SemaphoreType.DMA

    piece = ((2 * chunk, width), BF16)
    one = ((chunk, width), BF16)
    picked = call(
        functools.partial(pick_kernel, seq, images),
        [one] * (2 * seq),
        (tokens, cotangent),
        [dma((2 * seq,))],
        in_specs=[HBM] * 2,
        flops=1 << 34,
        name="pick",
    )
    toks, cots = picked[:seq], picked[seq:]
    error_rows = error_buffer.transpose(1, 0, 2)
    toks = [toks[0]] + [lax.ppermute(toks[k], "seq", flip(k, seq)) for k in range(seq - 1, 0, -1)]
    cots = [cots[0]] + [lax.ppermute(cots[k], "seq", flip(k, seq)) for k in range(seq - 1, 0, -1)]

    wide = ((rows, width), BF16)
    long = ((nkeys, width), BF16)
    probs = (HEADS, nkeys, rows)
    x_bf, query, keys, values, p_f, p_bf, resid, normed_two, w_down_t = call(
        functools.partial(forward_kernel, seq, images),
        [wide, wide, long, long, (probs, F32), (probs, BF16), ((rows, width), F32), wide, ((width, ff), BF16)],
        (
            *toks, key_mask, prompts, gain_one, shift_one, b_qkv, b_out, gain_two, shift_two,
            w_qkv, w_out, w_down,
        ),
        [
            pltpu.VMEM((rows, width), F32),
            pltpu.VMEM((seq, chunk, width), BF16),
            pltpu.VMEM((nkeys, width), BF16),
            pltpu.VMEM((nkeys, rows), F32),
            pltpu.VMEM((width, rows), BF16),
        ],
        flops=2 * rows * width * (4 * width + 2 * nkeys),
        vmem=8 * MIB,
        name="forward",
    )

    wire = BF16
    pgrad, act, dres, ds_bf, dmix = call(
        functools.partial(backward_kernel, seq, images),
        [
            ((pad, width), wire), ((rows, ff), BF16), ((rows, width), F32), (probs, BF16), wide,
        ],
        (
            *cots, query, values, p_f, p_bf, resid, normed_two, w_qkv, w_out, gain_two,
            w_up, b_up, w_down_t, prompts, gain_one,
        ),
        [
            pltpu.VMEM((rows, width), F32),
            pltpu.VMEM((seq, chunk, width), BF16),
            pltpu.VMEM((rows, ff), BF16),
            pltpu.VMEM((nkeys - rows, 2 * width), F32),
        ],
        flops=2 * rows * width * (3 * width + 3 * ff),
        vmem=8 * MIB,
        name="backward",
    )
    kept = (act, resid, dres, p_bf, ds_bf, query, dmix, keys, x_bf)

    (chunks,) = call(
        functools.partial(rest_kernel, seq),
        [((seq, 2 * chunk, width), BF16)],
        (*kept, w_down, w_qkv, b_down, gain_one),
        [
            pltpu.VMEM((rows, 3 * width), BF16),
            pltpu.VMEM((width, rows), BF16),
            pltpu.VMEM((rows, width), F32),
        ],
        flops=2 * rows * width * (3 * width + ff),
        vmem=8 * MIB,
        name="rest",
    )

    parts = [pgrad] + [lax.ppermute(pgrad, "seq", flip(k, seq)) for k in range(1, seq)]
    half = width // 2
    combined, keep, give = call(
        combine_kernel,
        [((pad, width), F32), ((pad, half), wire), ((pad, half), wire)],
        (error_rows, *parts, chunks),
        in_specs=[VMEM] * (1 + seq) + [ANY],
        name="combine",
    )
    parts = [keep, lax.ppermute(give, "dp", flip(1, dp))]
    if dp > 2:
        parts += [lax.ppermute(keep, "dp", flip(2, dp)), lax.ppermute(give, "dp", flip(3, dp))]
    bit = 4
    while bit < dp:
        (mine,) = call(add_kernel, [((pad, half), wire)], parts, name="add")
        parts = [mine, lax.ppermute(mine, "dp", flip(bit, dp))]
        bit *= 2
    (mine,) = call(add_kernel, [((pad, half), F32)], parts, name="add")
    other = lax.ppermute(mine, "dp", flip(1, dp))

    packs = call(
        functools.partial(pack_kernel, seq),
        [piece] * seq,
        (chunks, keep),
        in_specs=[VMEM, ANY],
        name="pack",
    )
    back = [packs[0]] + [lax.ppermute(packs[k], "seq", flip(k, seq)) for k in range(seq - 1, 0, -1)]

    rank = start_factor.shape[1]
    layer_out, input_grad, basis_t, right_t, error, new_momentum, new_prompts, prompt_copy = call(
        functools.partial(final_kernel, seq, images, images * dp),
        [
            ((images, chunk, width), BF16),
            ((images, chunk, width), BF16),
            ((rank, count), F32),
            ((rank, width), F32),
            ((count, 1, width), F32),
            ((count, width), F32),
            ((count, width), F32),
            ((count, width), BF16),
        ],
        (*back, mine, other, combined, start_factor.T, prompts, momentum),
        [pltpu.VMEM((pad, 2 * width), F32)],
        out_specs=[pl.BlockSpec(memory_space=pltpu.VMEM) for _ in range(8)],
        name="final",
    )
    return (
        layer_out,
        input_grad,
        basis_t.T,
        right_t.T,
        error.transpose(1, 0, 2),
        new_momentum,
        new_prompts,
        prompt_copy,
    )


def solution(mesh):
    rep = P()
    rows = P("dp", "seq", None)
    placed = (rows, P("dp", None), *([rep] * 13), rows, rep, P("dp", None, None), rep)
    return jax.shard_map(
        body,
        mesh=mesh,
        in_specs=placed,
        out_specs=(rows, rows, rep, rep, P("dp", None, None), rep, rep, rep),
        check_vma=False,
    )
```
